128 devices in a mesh: dp: 8 (over z, y_hi), fsdp: 16 (over y_lo, x, core).
Axes of the slice: x: 4, y: 4 (y_hi: 2, y_lo: 2; y = y_hi * 2 + y_lo), z: 4, core: 2. Of those that a mesh axis runs over, the one named last changes fastest.
Arguments:
- tokens: bfloat16 [16, 1024, 2048], P('dp', 'fsdp'), may hold values from -6 to 6
- w_qkv: bfloat16 [2048, 3072], P('fsdp', 'dp'), may hold values from -0.1875 to 0.1875
- w_out: bfloat16 [1024, 2048], P('fsdp', 'dp'), may hold values from -0.375 to 0.375
- ln_gain: float32 [2048], replicated, may hold values from 0.5 to 1.5
- ln_bias: float32 [2048], replicated, may hold values from -3 to 3
- kv_pool: bfloat16 [64, 128, 2048], P('fsdp'), may hold values from -300 to 300
- page_table: int32 [4, 16], replicated, may hold values from 0 to 63, as said below
- prefix_len: int32 [4], replicated, may hold values from 1 to 2048, as said below
- group_of: int32 [16], P('dp'), may hold values from 0 to 3, as said below
Outputs:
- hidden_out: bfloat16 [16, 1024, 2048], P('dp', 'fsdp')
- new_cache: bfloat16 [16, 1024, 2048], P('dp', 'fsdp')
The draws below stay inside these ranges and needn't reach their ends.
Inputs may be any that keep to these rules, and one draw needn't show every extreme that they name: `page_table`: a permutation of the pool's slots. `prefix_len`: some group's prefix is exactly 2048 long. `group_of`: each group has 4 requests.
All inputs are finite; a program needn't handle non-finite values.
Results may differ from the reference program's by a relative error of at most 0.012.
The reference program's roundings to bfloat16 on the way count: a program that leaves them out, or rounds other values in their place, can miss the bound.
Values may be sent and summed in bfloat16 or wider, within the bound.
A program may use at most 128 MiB of HBM per device.

```python
import jax
import jax.numpy as jnp
from jax import lax

D = 2048
HEADS = 8
HD = 128
PAGE = 128
PREFIX = 2048
GROUPS = 4
REQUESTS = 16
NEW = 1024
PAGES_MAX = 16
SLOTS = 64
N_FSDP = 16


def draw_page_table(key, part):
    order = jax.random.permutation(key, GROUPS * (PREFIX // PAGE))
    return order.astype(jnp.int32).reshape(GROUPS, PREFIX // PAGE)


def draw_prefix_len(key, part):
    first_key, second_key = jax.random.split(key)
    lengths = jax.random.randint(first_key, (GROUPS,), 1, PREFIX + 1)
    longest = jax.random.randint(second_key, (), 0, GROUPS)
    return jnp.where(jnp.arange(GROUPS) == longest, PREFIX, lengths).astype(jnp.int32)


def draw_group_of(key, part):
    order = jax.random.permutation(key, REQUESTS)
    return (order % GROUPS).astype(jnp.int32)


def draw_kv_pool(key, part):
    first_key = jax.random.fold_in(key, 0)
    inner = HEADS * HD
    base = jnp.clip(jax.random.normal(first_key, (SLOTS, PAGE, 2 * inner), jnp.float32), -6.0, 6.0) * 1.5
    return base.astype(jnp.bfloat16)


def level_of(stream_key, extent, cuts, smallest, top_value):
    factor_of, own = 1.0, jax.random.fold_in(stream_key, 6)
    for dim, shards_of in cuts:
        draws = jnp.exp(jax.random.uniform(jax.random.fold_in(own, dim), (shards_of,), jnp.float32, smallest / len(cuts), top_value / len(cuts)))
        factor_of = factor_of * jnp.repeat(draws, extent[dim] // shards_of).reshape([-1 if axis == dim else 1 for axis in range(len(extent))])
    return factor_of


def noise(key, extent, scale, reach, cuts=(), kind=jnp.bfloat16):
    loudness = level_of(key, extent, cuts, -0.22, 0.18) if cuts else 1.0
    result = jax.random.normal(key, extent, jnp.float32) * scale * loudness
    return jnp.minimum(jnp.maximum(result, -reach), reach).astype(kind)


def setup_inputs(seed: int = 0) -> dict:
    key_list = jax.random.split(jax.random.key(seed), 10)
    return {
        "tokens": noise(key_list[0], (REQUESTS, NEW, D), 1.0, 6.0, ((0, 8), (1, 16))),
        "w_qkv": noise(key_list[1], (D, 3 * HEADS * HD), (D // 2) ** -0.5, 0.1875, ((0, 16), (1, 8))),
        "w_out": noise(key_list[2], (HEADS * HD, D), (HEADS * HD // 4) ** -0.5, 0.375, ((0, 16), (1, 8))),
        "ln_gain": jnp.clip(1.0 + 0.1 * jax.random.normal(key_list[3], (D,), jnp.float32), 0.5, 1.5),
        "ln_bias": noise(key_list[4], (D,), 0.5, 3.0, (), jnp.float32),
        "kv_pool": draw_kv_pool(jax.random.fold_in(key_list[9], 71), 0),
        "page_table": draw_page_table(jax.random.fold_in(key_list[9], 71), 0),
        "prefix_len": draw_prefix_len(jax.random.fold_in(key_list[9], 71), 0),
        "group_of": draw_group_of(jax.random.fold_in(key_list[9], 71), 0),
    }


def reference(tokens, w_qkv, w_out, ln_gain, ln_bias, kv_pool, page_table, prefix_len, group_of):
    inner = HEADS * HD
    owner_slots = SLOTS // N_FSDP
    flat_rows = tokens.reshape(REQUESTS * NEW, D)
    qkv = jnp.dot(flat_rows, w_qkv, preferred_element_type=jnp.float32).astype(jnp.bfloat16)
    qkv = qkv.reshape(REQUESTS, NEW, 3 * inner)
    new_cache = qkv[:, :, inner:]
    slot_ids = jnp.arange(SLOTS, dtype=jnp.int32)
    matches = (page_table[:, :, None] == slot_ids[None, None, :]).astype(jnp.int32)
    slot_group = lax.optimization_barrier(jnp.sum(matches * jnp.arange(GROUPS, dtype=jnp.int32)[:, None, None], axis=(0, 1)))
    slot_page = lax.optimization_barrier(jnp.sum(matches * jnp.arange(PAGES_MAX, dtype=jnp.int32)[None, :, None], axis=(0, 1)))
    pool_pos = (slot_page[:, None] * PAGE + jnp.arange(PAGE, dtype=jnp.int32)[None, :]).reshape(N_FSDP, owner_slots * PAGE)
    pool_group = jnp.broadcast_to(slot_group[:, None], (SLOTS, PAGE)).reshape(N_FSDP, owner_slots * PAGE)
    pool_keys = kv_pool[:, :, :inner].reshape(N_FSDP, owner_slots * PAGE, HEADS, HD)
    pool_values = kv_pool[:, :, inner:].reshape(N_FSDP, owner_slots * PAGE, HEADS, HD)
    causal = jnp.arange(NEW, dtype=jnp.int32)[None, :] <= jnp.arange(NEW, dtype=jnp.int32)[:, None]
    inv_root = 1.0 / jnp.sqrt(jnp.float32(HD))

    def one_request(index):
        group = group_of[index]
        length = prefix_len[group]
        own_rows = qkv[index]
        query_rows = own_rows[:, :inner].reshape(NEW, HEADS, HD).astype(jnp.float32)

        def one_block(block):
            keys, values, positions, groups = block
            live = (groups == group) & (positions < length)
            scores = jnp.einsum('thd,khd->thk', query_rows, keys.astype(jnp.float32)) * inv_root
            scores = jnp.where(live[None, None, :], scores, -1e+30)
            row_max = lax.optimization_barrier(jnp.max(scores, axis=2))
            expo = jnp.where(live[None, None, :], jnp.exp(scores - row_max[:, :, None]), 0.0)
            row_total = lax.optimization_barrier(jnp.sum(expo, axis=2))
            weights = lax.optimization_barrier(expo.astype(jnp.bfloat16)).astype(jnp.float32)
            summed = jnp.einsum('thk,khd->thd', weights, values.astype(jnp.float32))
            normed = summed / jnp.maximum(row_total, 1.0)[:, :, None]
            normed = lax.optimization_barrier(normed.astype(jnp.bfloat16)).astype(jnp.float32)
            return (normed, row_max, row_total)
        part_norm, part_max, part_total = lax.map(one_block, (pool_keys, pool_values, pool_pos, pool_group))
        key_rows = own_rows[:, inner:2 * inner].reshape(NEW, HEADS, HD).astype(jnp.float32)
        value_rows = own_rows[:, 2 * inner:].reshape(NEW, HEADS, HD).astype(jnp.float32)
        scores = jnp.einsum('thd,khd->thk', query_rows, key_rows) * inv_root
        scores = jnp.where(causal[:, None, :], scores, -1e+30)
        new_max = lax.optimization_barrier(jnp.max(scores, axis=2))
        expo = jnp.where(causal[:, None, :], jnp.exp(scores - new_max[:, :, None]), 0.0)
        new_total = lax.optimization_barrier(jnp.sum(expo, axis=2))
        weights = lax.optimization_barrier(expo.astype(jnp.bfloat16)).astype(jnp.float32)
        new_sum = jnp.einsum('thk,khd->thd', weights, value_rows)
        overall = jnp.maximum(lax.optimization_barrier(jnp.max(part_max, axis=0)), new_max)
        factor = part_total * jnp.exp(part_max - overall[None])
        new_factor = jnp.exp(new_max - overall)
        numer = lax.optimization_barrier(jnp.sum(part_norm * factor[..., None], axis=0)) + new_sum * new_factor[..., None]
        denom = lax.optimization_barrier(jnp.sum(factor, axis=0)) + new_total * new_factor
        return (numer / denom[..., None]).reshape(NEW, inner).astype(jnp.bfloat16)
    attn = lax.map(one_request, jnp.arange(REQUESTS, dtype=jnp.int32))
    proj = jnp.dot(attn.reshape(REQUESTS * NEW, inner), w_out, preferred_element_type=jnp.float32)
    mixed = flat_rows.astype(jnp.float32) + proj
    mean_row = lax.optimization_barrier(jnp.mean(mixed, axis=1, keepdims=True))
    centred = mixed - mean_row
    var_row = lax.optimization_barrier(jnp.mean(centred * centred, axis=1, keepdims=True))
    normed = centred * lax.rsqrt(var_row + 1e-06) * ln_gain[None, :] + ln_bias[None, :]
    hidden_out = normed.astype(jnp.bfloat16).reshape(REQUESTS, NEW, D)
    return (hidden_out, new_cache)
```

```python
import functools
import math

import jax
import jax.numpy as jnp
from jax import lax
from jax.experimental import pallas as pl
from jax.experimental.pallas import tpu as pltpu
from jax.sharding import PartitionSpec as P

HD = 128
NEG = -1e30
LN_EPS = 1e-06
LOG2E = 1.4426950408889634

NN = (((1,), (0,)), ((), ()))
NT = (((1,), (1,)), ((), ()))
TN = (((0,), (0,)), ((), ()))


def dot32(a, b, dims):
    return lax.dot_general(a, b, dims, preferred_element_type=jnp.float32)


def fold8(x, op):
    out = x[0:8]
    for i in range(1, x.shape[0] // 8):
        out = op(out, x[8 * i : 8 * i + 8])
    return out


def attention_kernel(
    half_slots,
    page_table,
    prefix_len,
    group_of,
    q_ref,
    kn_ref,
    vn_ref,
    pool_ref,
    o1_ref,
    s1_ref,
    o2_ref,
    s2_ref,
    sc,
    scn,
    m_ref,
    l_ref,
    acc,
    slot_list,
    base_list,
):
    y = lax.axis_index("fsdp") // 8
    rows = q_ref.shape[1]
    page = pool_ref.shape[1]
    n_pages = page_table.shape[1]
    inv_root = 1.0 / math.sqrt(HD)
    key_iota = lax.broadcasted_iota(jnp.int32, (page, rows), 0)
    for j in range(2):
        req = y if j == 0 else 1 - y
        group = group_of[req]
        length = prefix_len[group]

        def build(p, count):
            loc = page_table[group, p] - half_slots * y
            live = (loc >= 0) & (loc < half_slots) & (p * page < length)

            @pl.when(live)
            def _():
                slot_list[count] = loc
                base_list[count] = p * page

            return count + live.astype(jnp.int32)

        count = lax.fori_loop(0, n_pages, build, jnp.int32(0))
        m_ref[...] = jnp.full(m_ref.shape, NEG, jnp.float32)
        l_ref[...] = jnp.zeros(l_ref.shape, jnp.float32)
        acc[...] = jnp.zeros(acc.shape, jnp.float32)
        q = q_ref[j]

        @pl.loop(0, count)
        def _(i):
            keys = pool_ref[slot_list[i], :, :HD]
            s = dot32(keys, q, NT) * inv_root
            s = jnp.where(key_iota < length - base_list[i], s, NEG)
            sc[i] = s
            m_ref[...] = jnp.maximum(m_ref[...], fold8(s, jnp.maximum))

        if j == 0:
            for kb in range(rows // page):
                lo = kb * page
                s = dot32(kn_ref[lo : lo + page, :], q[lo:, :], NT) * inv_root
                ki = lax.broadcasted_iota(jnp.int32, s.shape, 0)
                qi = lax.broadcasted_iota(jnp.int32, s.shape, 1)
                s = jnp.where(ki <= qi, s, NEG)
                scn[kb, :, lo:] = s
                m_ref[:, lo:] = jnp.maximum(m_ref[:, lo:], fold8(s, jnp.maximum))
        top = jnp.max(m_ref[...], axis=0, keepdims=True)

        @pl.loop(0, count)
        def _(i):
            e = jnp.exp2((sc[i] - top) * LOG2E)
            l_ref[...] += fold8(e, jnp.add)
            values = pool_ref[slot_list[i], :, HD:]
            acc[...] += dot32(values, e.astype(jnp.bfloat16), TN)

        if j == 0:
            for kb in range(rows // page):
                lo = kb * page
                e = jnp.exp2((scn[kb, :, lo:] - top[:, lo:]) * LOG2E)
                l_ref[:, lo:] += fold8(e, jnp.add)
                acc[:, lo:] += dot32(vn_ref[lo : lo + page, :], e.astype(jnp.bfloat16), TN)
        total = jnp.sum(l_ref[...], axis=0, keepdims=True)
        if j == 0:
            o1_ref[...] = acc[...]
            s1_ref[0:1, :] = top
            s1_ref[1:2, :] = total
            s1_ref[2:8, :] = jnp.zeros((6, rows), jnp.float32)
        else:
            o2_ref[...] = (acc[...] / jnp.maximum(total, 1.0)).astype(jnp.bfloat16)
            s2_ref[0:1, :] = top
            s2_ref[1:2, :] = total
            s2_ref[2:8, :] = jnp.zeros((6, rows), jnp.float32)


def attention(page_table, prefix_len, group_of, q2, k_new, v_new, pool):
    rows = q2.shape[1]
    slots, page = pool.shape[0], pool.shape[1]
    smem = pl.BlockSpec(memory_space=pltpu.SMEM)
    vmem = pl.BlockSpec(memory_space=pltpu.VMEM)
    return pl.pallas_call(
        functools.partial(attention_kernel, slots),
        out_shape=(
            jax.ShapeDtypeStruct((HD, rows), jnp.float32),
            jax.ShapeDtypeStruct((8, rows), jnp.float32),
            jax.ShapeDtypeStruct((HD, rows), jnp.bfloat16),
            jax.ShapeDtypeStruct((8, rows), jnp.float32),
        ),
        in_specs=[smem, smem, smem, vmem, vmem, vmem, vmem],
        out_specs=(vmem, vmem, vmem, vmem),
        scratch_shapes=[
            pltpu.VMEM((page_table.shape[1], page, rows), jnp.float32),
            pltpu.VMEM((rows // page, page, rows), jnp.float32),
            pltpu.VMEM((8, rows), jnp.float32),
            pltpu.VMEM((8, rows), jnp.float32),
            pltpu.VMEM((HD, rows), jnp.float32),
            pltpu.SMEM((page_table.shape[1],), jnp.int32),
            pltpu.SMEM((page_table.shape[1],), jnp.int32),
        ],
        compiler_params=pltpu.CompilerParams(vmem_limit_bytes=48 << 20),
        name="attend",
    )(page_table, prefix_len, group_of, q2, k_new, v_new, pool)


def body(tokens, w_qkv, w_out, ln_gain, ln_bias, kv_pool, page_table, prefix_len, group_of):
    reqs, toks, width = tokens.shape
    owners = lax.axis_size("fsdp")
    heads = owners // 2
    inner = heads * HD
    f = lax.axis_index("fsdp")
    y = f // heads
    rows = toks * owners
    rowsets = [list(range(heads)), list(range(heads, 2 * heads))]
    flip = [(i, (i + heads) % owners) for i in range(owners)]

    wall = lax.all_gather(w_qkv, "dp", axis=1, tiled=True)
    wh = wall.reshape(wall.shape[0], 3, heads, HD).transpose(2, 0, 1, 3)
    wh = wh.reshape(1, heads, wall.shape[0], 3 * HD)
    wh = jnp.concatenate([wh, wh], 0).reshape(owners, wall.shape[0], 3 * HD)
    wh = lax.all_to_all(wh, "fsdp", 0, 0, tiled=True).reshape(width, 3 * HD)
    sent = jnp.repeat(tokens, heads, axis=0)
    mine = lax.all_to_all(sent, "fsdp", 0, 0, tiled=True).reshape(rows, width)
    qkv = jnp.dot(mine, wh, preferred_element_type=jnp.float32).astype(jnp.bfloat16)
    q, k, v = qkv[:, :HD], qkv[:, HD : 2 * HD], qkv[:, 2 * HD :]

    kv = lax.all_to_all(
        qkv[:, HD:].reshape(owners, toks, 2 * HD), "fsdp", 0, 0, tiled=True
    )
    new_cache = (
        kv.reshape(2, heads, toks, 2, HD).transpose(0, 2, 3, 1, 4).reshape(2, toks, 2 * inner)
    )
    slots, page = kv_pool.shape[0], kv_pool.shape[1]
    ps = kv_pool.reshape(slots, page, 2, heads, HD).transpose(3, 0, 1, 2, 4)
    ps = lax.all_to_all(
        ps.reshape(heads, slots, page, 2 * HD), "fsdp", 0, 0, axis_index_groups=rowsets, tiled=True
    )
    pool = ps.reshape(heads * slots, page, 2 * HD)
    q_par = lax.ppermute(q, "fsdp", flip)
    o1, s1, o2, s2 = attention(
        page_table, prefix_len, group_of, jnp.stack([q, q_par]), k, v, pool
    )
    o2, s2 = lax.ppermute(o2, "fsdp", flip), lax.ppermute(s2, "fsdp", flip)
    top = jnp.maximum(s1[0], s2[0])
    f1 = jnp.exp(s1[0] - top)
    f2 = jnp.exp(s2[0] - top) * s2[1]
    attn = (o1 * f1 + o2.astype(jnp.float32) * f2) / (s1[1] * f1 + f2)
    attn = attn.T.astype(jnp.bfloat16).reshape(owners, toks, HD)
    attn = lax.all_to_all(attn, "fsdp", 0, 0, tiled=True)
    attn = attn.reshape(2, heads, toks, HD).transpose(0, 2, 1, 3).reshape(2 * toks, inner)

    wo = lax.all_gather(lax.all_gather(w_out, "dp", axis=1, tiled=True), "fsdp", axis=0, tiled=True)
    proj = jnp.dot(attn, wo, preferred_element_type=jnp.float32)
    mixed = tokens.reshape(reqs * toks, width).astype(jnp.float32) + proj
    centred = mixed - jnp.mean(mixed, axis=1, keepdims=True)
    var = jnp.mean(centred * centred, axis=1, keepdims=True)
    normed = centred * lax.rsqrt(var + LN_EPS) * ln_gain[None, :] + ln_bias[None, :]
    return normed.astype(jnp.bfloat16).reshape(reqs, toks, width), new_cache


def solution(mesh):
    in_specs = (
        P("dp", "fsdp", None),
        P("fsdp", "dp"),
        P("fsdp", "dp"),
        P(),
        P(),
        P("fsdp", None, None),
        P(),
        P(),
        P("dp"),
    )
    out_specs = (P("dp", "fsdp", None), P("dp", "fsdp", None))
    return jax.shard_map(body, mesh=mesh, in_specs=in_specs, out_specs=out_specs, check_vma=False)
```

```python
import functools
import math

import jax
import jax.numpy as jnp
from jax import lax
from jax.experimental import pallas as pl
from jax.experimental.pallas import tpu as pltpu
from jax.sharding import PartitionSpec as P

HD = 128
NEG = -1e30
LN_EPS = 1e-06
LOG2E = 1.4426950408889634

NN = (((1,), (0,)), ((), ()))
NT = (((1,), (1,)), ((), ()))
TN = (((0,), (0,)), ((), ()))


def dot32(a, b, dims):
    return lax.dot_general(a, b, dims, preferred_element_type=jnp.float32)


def fold8(x, op):
    out = x[0:8]
    for i in range(1, x.shape[0] // 8):
        out = op(out, x[8 * i : 8 * i + 8])
    return out


def attention_kernel(
    half_slots,
    page_table,
    prefix_len,
    group_of,
    q_ref,
    kn_ref,
    vn_ref,
    pool_ref,
    o1_ref,
    s1_ref,
    o2_ref,
    s2_ref,
    sc,
    scn,
    m_ref,
    l_ref,
    acc,
    slot_list,
    base_list,
):
    y = lax.axis_index("fsdp") // 8
    rows = q_ref.shape[1]
    page = pool_ref.shape[1]
    n_pages = page_table.shape[1]
    inv_root = 1.0 / math.sqrt(HD)
    key_iota = lax.broadcasted_iota(jnp.int32, (page, rows), 0)
    for j in range(2):
        req = y if j == 0 else 1 - y
        group = group_of[req]
        length = prefix_len[group]

        def build(p, count):
            loc = page_table[group, p] - half_slots * y
            live = (loc >= 0) & (loc < half_slots) & (p * page < length)

            @pl.when(live)
            def _():
                slot_list[count] = loc
                base_list[count] = p * page

            return count + live.astype(jnp.int32)

        count = lax.fori_loop(0, n_pages, build, jnp.int32(0))
        m_ref[...] = jnp.full(m_ref.shape, NEG, jnp.float32)
        l_ref[...] = jnp.zeros(l_ref.shape, jnp.float32)
        acc[...] = jnp.zeros(acc.shape, jnp.float32)
        q = q_ref[j]

        @pl.loop(0, count)
        def _(i):
            keys = pool_ref[slot_list[i], :, :HD]
            s = dot32(keys, q, NT) * inv_root
            s = jnp.where(key_iota < length - base_list[i], s, NEG)
            sc[i] = s
            m_ref[...] = jnp.maximum(m_ref[...], fold8(s, jnp.maximum))

        if j == 0:
            for kb in range(rows // page):
                lo = kb * page
                s = dot32(kn_ref[lo : lo + page, :], q[lo:, :], NT) * inv_root
                ki = lax.broadcasted_iota(jnp.int32, s.shape, 0)
                qi = lax.broadcasted_iota(jnp.int32, s.shape, 1)
                s = jnp.where(ki <= qi, s, NEG)
                scn[kb, :, lo:] = s
                m_ref[:, lo:] = jnp.maximum(m_ref[:, lo:], fold8(s, jnp.maximum))
        top = jnp.max(m_ref[...], axis=0, keepdims=True)

        @pl.loop(0, count)
        def _(i):
            e = jnp.exp2((sc[i] - top) * LOG2E)
            l_ref[...] += fold8(e, jnp.add)
            values = pool_ref[slot_list[i], :, HD:]
            acc[...] += dot32(values, e.astype(jnp.bfloat16), TN)

        if j == 0:
            for kb in range(rows // page):
                lo = kb * page
                e = jnp.exp2((scn[kb, :, lo:] - top[:, lo:]) * LOG2E)
                l_ref[:, lo:] += fold8(e, jnp.add)
                acc[:, lo:] += dot32(vn_ref[lo : lo + page, :], e.astype(jnp.bfloat16), TN)
        total = jnp.sum(l_ref[...], axis=0, keepdims=True)
        if j == 0:
            o1_ref[...] = acc[...]
            s1_ref[0:1, :] = top
            s1_ref[1:2, :] = total
            s1_ref[2:8, :] = jnp.zeros((6, rows), jnp.float32)
        else:
            o2_ref[...] = (acc[...] / jnp.maximum(total, 1.0)).astype(jnp.bfloat16)
            s2_ref[0:1, :] = top
            s2_ref[1:2, :] = total
            s2_ref[2:8, :] = jnp.zeros((6, rows), jnp.float32)


def attention(page_table, prefix_len, group_of, q2, k_new, v_new, pool):
    rows = q2.shape[1]
    slots, page = pool.shape[0], pool.shape[1]
    smem = pl.BlockSpec(memory_space=pltpu.SMEM)
    vmem = pl.BlockSpec(memory_space=pltpu.VMEM)
    return pl.pallas_call(
        functools.partial(attention_kernel, slots),
        out_shape=(
            jax.ShapeDtypeStruct((HD, rows), jnp.float32),
            jax.ShapeDtypeStruct((8, rows), jnp.float32),
            jax.ShapeDtypeStruct((HD, rows), jnp.bfloat16),
            jax.ShapeDtypeStruct((8, rows), jnp.float32),
        ),
        in_specs=[smem, smem, smem, vmem, vmem, vmem, vmem],
        out_specs=(vmem, vmem, vmem, vmem),
        scratch_shapes=[
            pltpu.VMEM((page_table.shape[1], page, rows), jnp.float32),
            pltpu.VMEM((rows // page, page, rows), jnp.float32),
            pltpu.VMEM((8, rows), jnp.float32),
            pltpu.VMEM((8, rows), jnp.float32),
            pltpu.VMEM((HD, rows), jnp.float32),
            pltpu.SMEM((page_table.shape[1],), jnp.int32),
            pltpu.SMEM((page_table.shape[1],), jnp.int32),
        ],
        compiler_params=pltpu.CompilerParams(vmem_limit_bytes=48 << 20),
        name="attend",
    )(page_table, prefix_len, group_of, q2, k_new, v_new, pool)


MESH = pl.DeviceIdType.MESH


class Copies:
    def __init__(self):
        self.started = []

    def send(self, src, dst, send_sem, recv_sem, device_id):
        copy = pltpu.make_async_remote_copy(
            src_ref=src,
            dst_ref=dst,
            send_sem=send_sem,
            recv_sem=recv_sem,
            device_id=device_id,
            device_id_type=MESH,
        )
        copy.start()
        self.started.append(copy)

    def finish(self):
        for copy in self.started:
            copy.wait_send()


def await_copy(dst, recv_sem):
    pltpu.make_async_copy(dst, dst, recv_sem).wait()


def front_kernel(
    tokens,
    w_ref,
    pool_in,
    q2,
    kv,
    pool,
    cache,
    x_buf,
    wall,
    wh,
    x_send,
    x_recv,
    w1_send,
    w1_recv,
    w2_send,
    w2_recv,
    w3_send,
    w3_recv,
    p_send,
    p_recv,
    c_send,
    c_recv,
    q_sem,
    local_sem,
):
    d = lax.axis_index("dp")
    f = lax.axis_index("fsdp")
    planes, owners = 8, 16
    heads = owners // 2
    y, h = f // heads, lax.rem(f, heads)
    x, core = h // 2, lax.rem(f, 2)
    toks = tokens.shape[1]
    wr = w_ref.shape[0]
    slots = pool_in.shape[0]

    def at(yy, xx, cc):
        return (yy * 4 + lax.rem(xx, 4)) * 2 + cc

    right, left = at(y, x + 1, core), at(y, x + 3, core)
    across, twin = at(1 - y, x, core), at(y, x, 1 - core)

    barrier = pltpu.get_barrier_semaphore()
    for k in range(1, owners):
        pl.semaphore_signal(
            barrier, inc=1, device_id={"fsdp": lax.rem(f + k, owners)}, device_id_type=MESH
        )
    for k in range(1, planes):
        pl.semaphore_signal(
            barrier, inc=1, device_id={"dp": lax.rem(d + k, planes)}, device_id_type=MESH
        )
    own_w = pltpu.make_async_copy(w_ref, wall.at[d], local_sem.at[0])
    own_w.start()
    own_x = pltpu.make_async_copy(tokens.at[y], x_buf.at[f], local_sem.at[1])
    own_x.start()
    pl.semaphore_wait(barrier, owners + planes - 2)

    out = Copies()
    for k in range(1, planes):
        out.send(
            w_ref, wall.at[d], w1_send.at[k - 1], w1_recv.at[d], {"dp": lax.rem(d + k, planes)}
        )

    def send_x(n, src, who, dest):
        out.send(src, x_buf.at[who], x_send.at[n], x_recv.at[who], {"fsdp": dest})

    send_x(0, tokens.at[1 - y], f, across)
    send_x(1, tokens.at[y], f, right)
    send_x(2, tokens.at[y], f, left)
    send_x(3, tokens.at[y], f, twin)

    for s in range(planes):

        @pl.when(d == s)
        def _():
            own_w.wait()

        @pl.when(d != s)
        def _():
            await_copy(wall.at[s], w1_recv.at[s])

        for j in range(3):
            t, head = divmod(3 * s + j, heads)
            src = wall.at[s, :, pl.ds(HD * j, HD)]
            dst = wh.at[f, :, pl.ds(HD * t, HD)]

            @pl.when(h == head)
            def _():
                pltpu.make_async_copy(src, dst, w2_recv.at[h, t]).start()

            @pl.when(h != head)
            def _():
                pltpu.make_async_remote_copy(
                    src_ref=src,
                    dst_ref=dst,
                    send_sem=w2_send.at[3 * s + j],
                    recv_sem=w2_recv.at[h, t],
                    device_id={"fsdp": y * heads + head},
                    device_id_type=MESH,
                ).start()

    await_copy(x_buf.at[across], x_recv.at[across])
    send_x(4, x_buf.at[across], across, right)
    send_x(5, x_buf.at[across], across, left)
    send_x(6, x_buf.at[across], across, twin)
    a_left, b_left = at(y, x + 3, core), at(1 - y, x + 3, core)
    a_right, b_right = at(y, x + 1, core), at(1 - y, x + 1, core)
    a_far, b_far = at(y, x + 2, core), at(1 - y, x + 2, core)
    await_copy(x_buf.at[a_left], x_recv.at[a_left])
    send_x(7, x_buf.at[a_left], a_left, right)
    send_x(8, x_buf.at[a_left], a_left, twin)
    await_copy(x_buf.at[a_right], x_recv.at[a_right])
    send_x(9, x_buf.at[a_right], a_right, twin)

    for r in range(heads):
        src = y * heads + r
        for t in range(3):
            part = wh.at[src, :, pl.ds(HD * t, HD)]
            await_copy(part, w2_recv.at[r, t])
        out.send(wh.at[src], wh.at[src], w3_send.at[r], w3_recv.at[r], {"fsdp": across})

    await_copy(x_buf.at[b_right], x_recv.at[b_right])
    send_x(10, x_buf.at[b_right], b_right, left)
    send_x(11, x_buf.at[b_right], b_right, twin)
    await_copy(x_buf.at[b_left], x_recv.at[b_left])
    send_x(12, x_buf.at[b_left], b_left, twin)

    own_pool = []
    for k in range(heads):
        head = lax.rem(h + k, heads)
        for t in range(2):
            cols = pl.ds(pl.multiple_of((t * heads + head) * HD, HD), HD)
            src = pool_in.at[:, :, cols]
            dst = pool.at[pl.ds(h * slots, slots), :, pl.ds(t * HD, HD)]
            if k == 0:
                copy = pltpu.make_async_copy(src, dst, local_sem.at[2 + t])
                copy.start()
                own_pool.append(copy)
            else:
                out.send(
                    src, dst, p_send.at[k, t], p_recv.at[h, t], {"fsdp": y * heads + head}
                )

    await_copy(x_buf.at[a_far], x_recv.at[a_far])
    send_x(13, x_buf.at[a_far], a_far, twin)
    await_copy(x_buf.at[b_far], x_recv.at[b_far])
    send_x(14, x_buf.at[b_far], b_far, twin)
    for yy in range(2):
        for xx in range(4):
            who = at(yy, xx, 1 - core)
            await_copy(x_buf.at[who], x_recv.at[who])
    own_x.wait()
    for r in range(heads):
        src = (1 - y) * heads + r
        await_copy(wh.at[src], w3_recv.at[r])

    @pl.loop(0, owners // 4)
    def _(i):
        left_rows = x_buf[pl.ds(4 * i, 4)].reshape(4 * toks, owners * wr)
        got = dot32(left_rows, wh[...].reshape(owners * wr, 3 * HD), NN).astype(jnp.bfloat16)
        q2[0, pl.ds(pl.multiple_of(4 * i * toks, 4 * toks), 4 * toks), :] = got[:, :HD]
        kv[pl.ds(4 * i, 4)] = got[:, HD:].reshape(4, toks, 2 * HD)

    out.send(q2.at[0], q2.at[1], q_sem.at[0], q_sem.at[1], {"fsdp": across})
    own_cache = []
    for k in range(owners):
        who = lax.rem(f + k, owners)
        for t in range(2):
            cols = pl.ds(pl.multiple_of((t * heads + h) * HD, HD), HD)
            src = kv.at[who, :, pl.ds(t * HD, HD)]
            dst = cache.at[y, :, cols]
            if k == 0:
                copy = pltpu.make_async_copy(src, dst, local_sem.at[4 + t])
                copy.start()
                own_cache.append(copy)
            else:
                out.send(src, dst, c_send.at[k, t], c_recv.at[f, t], {"fsdp": who})

    await_copy(q2.at[1], q_sem.at[1])
    for copy in own_pool + own_cache:
        copy.wait()
    for k in range(1, heads):
        who = lax.rem(h + k, heads)
        for t in range(2):
            await_copy(
                pool.at[pl.ds(who * slots, slots), :, pl.ds(t * HD, HD)], p_recv.at[who, t]
            )
    for k in range(1, owners):
        who = lax.rem(f + k, owners)
        for t in range(2):
            cols = pl.ds(pl.multiple_of((t * heads + lax.rem(who, heads)) * HD, HD), HD)
            await_copy(cache.at[who // heads, :, cols], c_recv.at[who, t])
    for s in range(planes):
        for j in range(3):
            head = (3 * s + j) % heads

            @pl.when(h != head)
            def _():
                part = wall.at[s, :, pl.ds(HD * j, HD)]
                await_copy(part, w2_send.at[3 * s + j])

    out.finish()


def front(tokens, w_qkv, kv_pool):
    reqs, toks, width = tokens.shape
    slots, page, _ = kv_pool.shape
    owners, planes, heads = 16, 8, 8
    dma = pltpu.SemaphoreType.DMA
    hbm = pl.BlockSpec(memory_space=pl.ANY)
    vmem = pl.BlockSpec(memory_space=pltpu.VMEM)
    bf16 = jnp.bfloat16
    return pl.pallas_call(
        front_kernel,
        out_shape=(
            jax.ShapeDtypeStruct((2, owners * toks, HD), bf16),
            jax.ShapeDtypeStruct((owners, toks, 2 * HD), bf16),
            jax.ShapeDtypeStruct((heads * slots, page, 2 * HD), bf16),
            jax.ShapeDtypeStruct((reqs, toks, 2 * heads * HD), bf16),
        ),
        in_specs=[hbm, hbm, hbm],
        out_specs=(vmem, vmem, hbm, hbm),
        scratch_shapes=[
            pltpu.VMEM((owners, toks, width), bf16),
            pltpu.VMEM((planes,) + w_qkv.shape, bf16),
            pltpu.VMEM((owners, w_qkv.shape[0], 3 * HD), bf16),
            dma((15,)),
            dma((owners,)),
            dma((planes - 1,)),
            dma((planes,)),
            dma((3 * planes,)),
            dma((heads, 3)),
            dma((heads,)),
            dma((heads,)),
            dma((heads, 2)),
            dma((heads, 2)),
            dma((owners, 2)),
            dma((owners, 2)),
            dma((2,)),
            dma((6,)),
        ],
        compiler_params=pltpu.CompilerParams(
            collective_id=0, has_side_effects=True, vmem_limit_bytes=40 << 20
        ),
        name="front",
    )(tokens, w_qkv, kv_pool)


def body(tokens, w_qkv, w_out, ln_gain, ln_bias, kv_pool, page_table, prefix_len, group_of):
    reqs, toks, width = tokens.shape
    owners = lax.axis_size("fsdp")
    heads = owners // 2
    inner = heads * HD
    rows = toks * owners
    flip = [(i, (i + heads) % owners) for i in range(owners)]

    q2, kv, pool, new_cache = front(tokens, w_qkv, kv_pool)
    kv = kv.reshape(rows, 2 * HD)
    k, v = kv[:, :HD], kv[:, HD:]
    o1, s1, o2, s2 = attention(
        page_table, prefix_len, group_of, q2, k, v, pool
    )
    o2, s2 = lax.ppermute(o2, "fsdp", flip), lax.ppermute(s2, "fsdp", flip)
    top = jnp.maximum(s1[0], s2[0])
    f1 = jnp.exp(s1[0] - top)
    f2 = jnp.exp(s2[0] - top) * s2[1]
    attn = (o1 * f1 + o2.astype(jnp.float32) * f2) / (s1[1] * f1 + f2)
    attn = attn.T.astype(jnp.bfloat16).reshape(owners, toks, HD)
    attn = lax.all_to_all(attn, "fsdp", 0, 0, tiled=True)
    attn = attn.reshape(2, heads, toks, HD).transpose(0, 2, 1, 3).reshape(2 * toks, inner)

    wo = lax.all_gather(lax.all_gather(w_out, "dp", axis=1, tiled=True), "fsdp", axis=0, tiled=True)
    proj = jnp.dot(attn, wo, preferred_element_type=jnp.float32)
    mixed = tokens.reshape(reqs * toks, width).astype(jnp.float32) + proj
    centred = mixed - jnp.mean(mixed, axis=1, keepdims=True)
    var = jnp.mean(centred * centred, axis=1, keepdims=True)
    normed = centred * lax.rsqrt(var + LN_EPS) * ln_gain[None, :] + ln_bias[None, :]
    return normed.astype(jnp.bfloat16).reshape(reqs, toks, width), new_cache


def solution(mesh):
    in_specs = (
        P("dp", "fsdp", None),
        P("fsdp", "dp"),
        P("fsdp", "dp"),
        P(),
        P(),
        P("fsdp", None, None),
        P(),
        P(),
        P("dp"),
    )
    out_specs = (P("dp", "fsdp", None), P("dp", "fsdp", None))
    return jax.shard_map(body, mesh=mesh, in_specs=in_specs, out_specs=out_specs, check_vma=False)
```

```python
import functools
import math

import jax
import jax.numpy as jnp
from jax import lax
from jax.experimental import pallas as pl
from jax.experimental.pallas import tpu as pltpu
from jax.sharding import PartitionSpec as P

HD = 128
NEG = -1e30
LN_EPS = 1e-06
LOG2E = 1.4426950408889634

NN = (((1,), (0,)), ((), ()))
NT = (((1,), (1,)), ((), ()))
TN = (((0,), (0,)), ((), ()))


def dot32(a, b, dims):
    return lax.dot_general(a, b, dims, preferred_element_type=jnp.float32)


def fold8(x, op):
    out = x[0:8]
    for i in range(1, x.shape[0] // 8):
        out = op(out, x[8 * i : 8 * i + 8])
    return out


def attention_kernel(
    half_slots,
    page_table,
    prefix_len,
    group_of,
    q_ref,
    kn_ref,
    vn_ref,
    pool_ref,
    o1_ref,
    s1_ref,
    o2_ref,
    s2_ref,
    sc,
    scn,
    m_ref,
    l_ref,
    acc,
    slot_list,
    base_list,
):
    y = lax.axis_index("fsdp") // 8
    rows = q_ref.shape[1]
    page = pool_ref.shape[1]
    n_pages = page_table.shape[1]
    inv_root = 1.0 / math.sqrt(HD)
    key_iota = lax.broadcasted_iota(jnp.int32, (page, rows), 0)
    for j in range(2):
        req = y if j == 0 else 1 - y
        group = group_of[req]
        length = prefix_len[group]

        def build(p, count):
            loc = page_table[group, p] - half_slots * y
            live = (loc >= 0) & (loc < half_slots) & (p * page < length)

            @pl.when(live)
            def _():
                slot_list[count] = loc
                base_list[count] = p * page

            return count + live.astype(jnp.int32)

        count = lax.fori_loop(0, n_pages, build, jnp.int32(0))
        m_ref[...] = jnp.full(m_ref.shape, NEG, jnp.float32)
        l_ref[...] = jnp.zeros(l_ref.shape, jnp.float32)
        acc[...] = jnp.zeros(acc.shape, jnp.float32)
        q = q_ref[j]

        @pl.loop(0, count)
        def _(i):
            keys = pool_ref[slot_list[i], :, :HD]
            s = dot32(keys, q, NT) * inv_root
            s = jnp.where(key_iota < length - base_list[i], s, NEG)
            sc[i] = s
            m_ref[...] = jnp.maximum(m_ref[...], fold8(s, jnp.maximum))

        if j == 0:
            for kb in range(rows // page):
                lo = kb * page
                s = dot32(kn_ref[lo : lo + page, :], q[lo:, :], NT) * inv_root
                ki = lax.broadcasted_iota(jnp.int32, s.shape, 0)
                qi = lax.broadcasted_iota(jnp.int32, s.shape, 1)
                s = jnp.where(ki <= qi, s, NEG)
                scn[kb, :, lo:] = s
                m_ref[:, lo:] = jnp.maximum(m_ref[:, lo:], fold8(s, jnp.maximum))
        top = jnp.max(m_ref[...], axis=0, keepdims=True)

        @pl.loop(0, count)
        def _(i):
            e = jnp.exp2((sc[i] - top) * LOG2E)
            l_ref[...] += fold8(e, jnp.add)
            values = pool_ref[slot_list[i], :, HD:]
            acc[...] += dot32(values, e.astype(jnp.bfloat16), TN)

        if j == 0:
            for kb in range(rows // page):
                lo = kb * page
                e = jnp.exp2((scn[kb, :, lo:] - top[:, lo:]) * LOG2E)
                l_ref[:, lo:] += fold8(e, jnp.add)
                acc[:, lo:] += dot32(vn_ref[lo : lo + page, :], e.astype(jnp.bfloat16), TN)
        total = jnp.sum(l_ref[...], axis=0, keepdims=True)
        if j == 0:
            o1_ref[...] = acc[...]
            s1_ref[0:1, :] = top
            s1_ref[1:2, :] = total
            s1_ref[2:8, :] = jnp.zeros((6, rows), jnp.float32)
        else:
            o2_ref[...] = (acc[...] / jnp.maximum(total, 1.0)).astype(jnp.bfloat16)
            s2_ref[0:1, :] = top
            s2_ref[1:2, :] = total
            s2_ref[2:8, :] = jnp.zeros((6, rows), jnp.float32)


def attention(page_table, prefix_len, group_of, q2, k_new, v_new, pool):
    rows = q2.shape[1]
    slots, page = pool.shape[0], pool.shape[1]
    smem = pl.BlockSpec(memory_space=pltpu.SMEM)
    vmem = pl.BlockSpec(memory_space=pltpu.VMEM)
    return pl.pallas_call(
        functools.partial(attention_kernel, slots),
        out_shape=(
            jax.ShapeDtypeStruct((HD, rows), jnp.float32),
            jax.ShapeDtypeStruct((8, rows), jnp.float32),
            jax.ShapeDtypeStruct((HD, rows), jnp.bfloat16),
            jax.ShapeDtypeStruct((8, rows), jnp.float32),
        ),
        in_specs=[smem, smem, smem, vmem, vmem, vmem, vmem],
        out_specs=(vmem, vmem, vmem, vmem),
        scratch_shapes=[
            pltpu.VMEM((page_table.shape[1], page, rows), jnp.float32),
            pltpu.VMEM((rows // page, page, rows), jnp.float32),
            pltpu.VMEM((8, rows), jnp.float32),
            pltpu.VMEM((8, rows), jnp.float32),
            pltpu.VMEM((HD, rows), jnp.float32),
            pltpu.SMEM((page_table.shape[1],), jnp.int32),
            pltpu.SMEM((page_table.shape[1],), jnp.int32),
        ],
        compiler_params=pltpu.CompilerParams(vmem_limit_bytes=48 << 20),
        name="attend",
    )(page_table, prefix_len, group_of, q2, k_new, v_new, pool)


MESH = pl.DeviceIdType.MESH


class Copies:
    def __init__(self):
        self.started = []

    def send(self, src, dst, send_sem, recv_sem, device_id):
        copy = pltpu.make_async_remote_copy(
            src_ref=src,
            dst_ref=dst,
            send_sem=send_sem,
            recv_sem=recv_sem,
            device_id=device_id,
            device_id_type=MESH,
        )
        copy.start()
        self.started.append(copy)

    def finish(self):
        for copy in self.started:
            copy.wait_send()


def await_copy(dst, recv_sem):
    pltpu.make_async_copy(dst, dst, recv_sem).wait()


def front_kernel(
    tokens,
    w_ref,
    wo_ref,
    pool_in,
    q2,
    kv,
    pool,
    cache,
    wo,
    x_buf,
    wall,
    wh,
    x_send,
    x_recv,
    w1_send,
    w1_recv,
    w2_send,
    w2_recv,
    w3_send,
    w3_recv,
    p_send,
    p_recv,
    c_send,
    c_recv,
    q_sem,
    local_sem,
    o1_send,
    o1_recv,
    o2_send,
    o2_recv,
):
    d = lax.axis_index("dp")
    f = lax.axis_index("fsdp")
    planes, owners = 8, 16
    heads = owners // 2
    y, h = f // heads, lax.rem(f, heads)
    x, core = h // 2, lax.rem(f, 2)
    toks = tokens.shape[1]
    wr = w_ref.shape[0]
    slots = pool_in.shape[0]

    def at(yy, xx, cc):
        return (yy * 4 + lax.rem(xx, 4)) * 2 + cc

    right, left = at(y, x + 1, core), at(y, x + 3, core)
    across, twin = at(1 - y, x, core), at(y, x, 1 - core)

    barrier = pltpu.get_barrier_semaphore()
    for k in range(1, owners):
        pl.semaphore_signal(
            barrier, inc=1, device_id={"fsdp": lax.rem(f + k, owners)}, device_id_type=MESH
        )
    for k in range(1, planes):
        pl.semaphore_signal(
            barrier, inc=1, device_id={"dp": lax.rem(d + k, planes)}, device_id_type=MESH
        )
    z, z_pair = d // 2, lax.rem(d, 2)
    other_plane = 2 * z + 1 - z_pair
    for k in range(1, owners):
        pl.semaphore_signal(
            barrier,
            inc=1,
            device_id={"dp": other_plane, "fsdp": lax.rem(f + k, owners)},
            device_id_type=MESH,
        )
    own_w = pltpu.make_async_copy(w_ref, wall.at[d], local_sem.at[0])
    own_w.start()
    own_x = pltpu.make_async_copy(tokens.at[y], x_buf.at[f], local_sem.at[1])
    own_x.start()
    pl.semaphore_wait(barrier, 2 * owners + planes - 3)

    out = Copies()
    for k in range(1, planes):
        out.send(
            w_ref, wall.at[d], w1_send.at[k - 1], w1_recv.at[d], {"dp": lax.rem(d + k, planes)}
        )

    def send_x(n, src, who, dest):
        out.send(src, x_buf.at[who], x_send.at[n], x_recv.at[who], {"fsdp": dest})

    send_x(0, tokens.at[1 - y], f, across)
    send_x(1, tokens.at[y], f, right)
    send_x(2, tokens.at[y], f, left)
    send_x(3, tokens.at[y], f, twin)

    group = f // heads
    for p in range(2):
        for k in range(heads):
            dest = lax.rem(f // 2 + k, heads) * 2 + z_pair
            plane = d if p == 0 else other_plane
            sem = o1_send.at[p * heads + k]
            dst = wo.at[d, f]
            if p == 0 and k == 0:

                @pl.when(core == z_pair)
                def _():
                    pltpu.make_async_copy(wo_ref, dst, o1_recv.at[group]).start()

                @pl.when(core != z_pair)
                def _():
                    pltpu.make_async_remote_copy(
                        src_ref=wo_ref,
                        dst_ref=dst,
                        send_sem=sem,
                        recv_sem=o1_recv.at[group],
                        device_id={"fsdp": dest},
                        device_id_type=MESH,
                    ).start()

            else:
                out.send(wo_ref, dst, sem, o1_recv.at[group], {"dp": plane, "fsdp": dest})

    for s in range(planes):

        @pl.when(d == s)
        def _():
            own_w.wait()

        @pl.when(d != s)
        def _():
            await_copy(wall.at[s], w1_recv.at[s])

        for j in range(3):
            t, head = divmod(3 * s + j, heads)
            src = wall.at[s, :, pl.ds(HD * j, HD)]
            dst = wh.at[f, :, pl.ds(HD * t, HD)]

            @pl.when(h == head)
            def _():
                pltpu.make_async_copy(src, dst, w2_recv.at[h, t]).start()

            @pl.when(h != head)
            def _():
                pltpu.make_async_remote_copy(
                    src_ref=src,
                    dst_ref=dst,
                    send_sem=w2_send.at[3 * s + j],
                    recv_sem=w2_recv.at[h, t],
                    device_id={"fsdp": y * heads + head},
                    device_id_type=MESH,
                ).start()

    await_copy(x_buf.at[across], x_recv.at[across])
    send_x(4, x_buf.at[across], across, right)
    send_x(5, x_buf.at[across], across, left)
    send_x(6, x_buf.at[across], across, twin)
    a_left, b_left = at(y, x + 3, core), at(1 - y, x + 3, core)
    a_right, b_right = at(y, x + 1, core), at(1 - y, x + 1, core)
    a_far, b_far = at(y, x + 2, core), at(1 - y, x + 2, core)
    await_copy(x_buf.at[a_left], x_recv.at[a_left])
    send_x(7, x_buf.at[a_left], a_left, right)
    send_x(8, x_buf.at[a_left], a_left, twin)
    await_copy(x_buf.at[a_right], x_recv.at[a_right])
    send_x(9, x_buf.at[a_right], a_right, twin)

    for r in range(heads):
        src = y * heads + r
        for t in range(3):
            part = wh.at[src, :, pl.ds(HD * t, HD)]
            await_copy(part, w2_recv.at[r, t])
        out.send(wh.at[src], wh.at[src], w3_send.at[r], w3_recv.at[r], {"fsdp": across})

    await_copy(x_buf.at[b_right], x_recv.at[b_right])
    send_x(10, x_buf.at[b_right], b_right, left)
    send_x(11, x_buf.at[b_right], b_right, twin)
    await_copy(x_buf.at[b_left], x_recv.at[b_left])
    send_x(12, x_buf.at[b_left], b_left, twin)

    def half(plane, n):
        return wo.at[plane, pl.ds(n * heads, heads)]

    def send_o(n, plane, part, dp, ff):
        out.send(
            half(plane, part),
            half(plane, part),
            o2_send.at[n],
            o2_recv.at[plane, part],
            {"dp": dp, "fsdp": ff},
        )

    def z_plane(k, c):
        return 2 * lax.rem(z + k, 4) + c

    up, down = z_plane(1, z_pair), z_plane(3, z_pair)
    for part in range(2):
        await_copy(half(z_plane(0, core), part), o1_recv.at[part])
        send_o(3 * part, z_plane(0, core), part, up, f)
        send_o(3 * part + 1, z_plane(0, core), part, down, f)
        send_o(3 * part + 2, z_plane(0, core), part, d, twin)

    own_pool = []
    for k in range(heads):
        head = lax.rem(h + k, heads)
        for t in range(2):
            cols = pl.ds(pl.multiple_of((t * heads + head) * HD, HD), HD)
            src = pool_in.at[:, :, cols]
            dst = pool.at[pl.ds(h * slots, slots), :, pl.ds(t * HD, HD)]
            if k == 0:
                copy = pltpu.make_async_copy(src, dst, local_sem.at[2 + t])
                copy.start()
                own_pool.append(copy)
            else:
                out.send(
                    src, dst, p_send.at[k, t], p_recv.at[h, t], {"fsdp": y * heads + head}
                )

    for n, (k, part) in enumerate(((3, 0), (1, 1), (1, 0), (3, 1))):
        plane = z_plane(k, core)
        await_copy(half(plane, part), o2_recv.at[plane, part])
        if n == 0:
            send_o(6, plane, part, up, f)
        if n == 1:
            send_o(7, plane, part, down, f)
        send_o(8 + n, plane, part, d, twin)

    await_copy(x_buf.at[a_far], x_recv.at[a_far])
    send_x(13, x_buf.at[a_far], a_far, twin)
    await_copy(x_buf.at[b_far], x_recv.at[b_far])
    send_x(14, x_buf.at[b_far], b_far, twin)
    for yy in range(2):
        for xx in range(4):
            who = at(yy, xx, 1 - core)
            await_copy(x_buf.at[who], x_recv.at[who])
    own_x.wait()
    for r in range(heads):
        src = (1 - y) * heads + r
        await_copy(wh.at[src], w3_recv.at[r])

    @pl.loop(0, owners // 4)
    def _(i):
        left_rows = x_buf[pl.ds(4 * i, 4)].reshape(4 * toks, owners * wr)
        got = dot32(left_rows, wh[...].reshape(owners * wr, 3 * HD), NN).astype(jnp.bfloat16)
        q2[0, pl.ds(pl.multiple_of(4 * i * toks, 4 * toks), 4 * toks), :] = got[:, :HD]
        kv[pl.ds(4 * i, 4)] = got[:, HD:].reshape(4, toks, 2 * HD)

    out.send(q2.at[0], q2.at[1], q_sem.at[0], q_sem.at[1], {"fsdp": across})
    own_cache = []
    for k in range(owners):
        who = lax.rem(f + k, owners)
        for t in range(2):
            cols = pl.ds(pl.multiple_of((t * heads + h) * HD, HD), HD)
            src = kv.at[who, :, pl.ds(t * HD, HD)]
            dst = cache.at[y, :, cols]
            if k == 0:
                copy = pltpu.make_async_copy(src, dst, local_sem.at[4 + t])
                copy.start()
                own_cache.append(copy)
            else:
                out.send(src, dst, c_send.at[k, t], c_recv.at[f, t], {"fsdp": who})

    for part in range(2):
        plane = z_plane(2, core)
        await_copy(half(plane, part), o2_recv.at[plane, part])
        send_o(12 + part, plane, part, d, twin)
    for k in range(4):
        for part in range(2):
            plane = z_plane(k, 1 - core)
            await_copy(half(plane, part), o2_recv.at[plane, part])

    @pl.when(core != z_pair)
    def _():
        await_copy(wo.at[d, f], o1_send.at[0])

    await_copy(q2.at[1], q_sem.at[1])
    for copy in own_pool + own_cache:
        copy.wait()
    for k in range(1, heads):
        who = lax.rem(h + k, heads)
        for t in range(2):
            await_copy(
                pool.at[pl.ds(who * slots, slots), :, pl.ds(t * HD, HD)], p_recv.at[who, t]
            )
    for k in range(1, owners):
        who = lax.rem(f + k, owners)
        for t in range(2):
            cols = pl.ds(pl.multiple_of((t * heads + lax.rem(who, heads)) * HD, HD), HD)
            await_copy(cache.at[who // heads, :, cols], c_recv.at[who, t])
    for s in range(planes):
        for j in range(3):
            head = (3 * s + j) % heads

            @pl.when(h != head)
            def _():
                part = wall.at[s, :, pl.ds(HD * j, HD)]
                await_copy(part, w2_send.at[3 * s + j])

    out.finish()


def front(tokens, w_qkv, w_out, kv_pool):
    reqs, toks, width = tokens.shape
    slots, page, _ = kv_pool.shape
    owners, planes, heads = 16, 8, 8
    dma = pltpu.SemaphoreType.DMA
    hbm = pl.BlockSpec(memory_space=pl.ANY)
    vmem = pl.BlockSpec(memory_space=pltpu.VMEM)
    bf16 = jnp.bfloat16
    return pl.pallas_call(
        front_kernel,
        out_shape=(
            jax.ShapeDtypeStruct((2, owners * toks, HD), bf16),
            jax.ShapeDtypeStruct((owners, toks, 2 * HD), bf16),
            jax.ShapeDtypeStruct((heads * slots, page, 2 * HD), bf16),
            jax.ShapeDtypeStruct((reqs, toks, 2 * heads * HD), bf16),
            jax.ShapeDtypeStruct((planes, owners) + w_out.shape, bf16),
        ),
        in_specs=[hbm, hbm, hbm, hbm],
        out_specs=(vmem, vmem, hbm, hbm, hbm),
        scratch_shapes=[
            pltpu.VMEM((owners, toks, width), bf16),
            pltpu.VMEM((planes,) + w_qkv.shape, bf16),
            pltpu.VMEM((owners, w_qkv.shape[0], 3 * HD), bf16),
            dma((15,)),
            dma((owners,)),
            dma((planes - 1,)),
            dma((planes,)),
            dma((3 * planes,)),
            dma((heads, 3)),
            dma((heads,)),
            dma((heads,)),
            dma((heads, 2)),
            dma((heads, 2)),
            dma((owners, 2)),
            dma((owners, 2)),
            dma((2,)),
            dma((6,)),
            dma((owners,)),
            dma((2,)),
            dma((15,)),
            dma((planes, 2)),
        ],
        compiler_params=pltpu.CompilerParams(
            collective_id=0, has_side_effects=True, vmem_limit_bytes=40 << 20
        ),
        name="front",
    )(tokens, w_qkv, w_out, kv_pool)


def tail_kernel(
    tokens,
    o1,
    s1,
    o2,
    s2,
    wo_hbm,
    gain,
    bias,
    hidden,
    o2_in,
    s2_in,
    at_out,
    at_in,
    wo,
    mixed,
    y_send,
    y_recv,
    a_send,
    a_recv,
    w_sem,
):
    f = lax.axis_index("fsdp")
    owners = 16
    heads = owners // 2
    y, h = f // heads, lax.rem(f, heads)
    across = (1 - y) * heads + h
    planes, depth, cols = wo.shape
    reqs, toks, width = tokens.shape
    rows = owners * toks

    barrier = pltpu.get_barrier_semaphore()
    for k in range(1, owners):
        pl.semaphore_signal(
            barrier, inc=1, device_id={"fsdp": lax.rem(f + k, owners)}, device_id_type=MESH
        )
    loads = []
    for p in range(planes):
        load = pltpu.make_async_copy(wo_hbm.at[p], wo.at[p], w_sem.at[p])
        load.start()
        loads.append(load)
    pl.semaphore_wait(barrier, owners - 1)
    out = Copies()
    out.send(s2, s2_in, y_send.at[0], y_recv.at[0], {"fsdp": across})
    out.send(o2, o2_in, y_send.at[1], y_recv.at[1], {"fsdp": across})
    await_copy(s2_in, y_recv.at[0])
    top = jnp.maximum(s1[0:1, :], s2_in[0:1, :])
    f1 = jnp.exp(s1[0:1, :] - top)
    f2 = jnp.exp(s2_in[0:1, :] - top) * s2_in[1:2, :]
    denom = s1[1:2, :] * f1 + f2
    await_copy(o2_in, y_recv.at[1])
    attn = (o1[...] * f1 + o2_in[...].astype(jnp.float32) * f2) / denom
    at_out[...] = attn.T.astype(jnp.bfloat16).reshape(owners, toks, HD)
    at_in[y, :, pl.ds(pl.multiple_of(h * HD, HD), HD)] = at_out[f]
    for k in range(1, owners):
        who = lax.rem(f + k, owners)
        dst = at_in.at[y, :, pl.ds(pl.multiple_of(h * HD, HD), HD)]
        out.send(at_out.at[who], dst, a_send.at[k], a_recv.at[f], {"fsdp": who})
    for k in range(1, owners):
        who = lax.rem(f + k, owners)
        col = pl.multiple_of(lax.rem(who, heads) * HD, HD)
        await_copy(at_in.at[who // heads, :, pl.ds(col, HD)], a_recv.at[who])
    left_rows = at_in[...].reshape(reqs * toks, depth)
    total = jnp.zeros((reqs * toks, 1), jnp.float32)
    for p in range(planes):
        loads[p].wait()
        part = dot32(left_rows, wo[p], NN)
        part = part + tokens[:, :, p * cols : (p + 1) * cols].reshape(
            reqs * toks, cols
        ).astype(jnp.float32)
        total = total + jnp.sum(part, axis=1, keepdims=True)
        mixed[:, p * cols : (p + 1) * cols] = part
    mean = total * (1.0 / width)
    square = jnp.zeros((reqs * toks, 1), jnp.float32)
    for p in range(planes):
        centred = mixed[:, p * cols : (p + 1) * cols] - mean
        square = square + jnp.sum(centred * centred, axis=1, keepdims=True)
    scale = lax.rsqrt(square * (1.0 / width) + LN_EPS)
    for p in range(planes):
        at = slice(p * cols, (p + 1) * cols)
        normed = (mixed[:, at] - mean) * scale * gain[0:1, at] + bias[0:1, at]
        hidden[:, :, at] = normed.astype(jnp.bfloat16).reshape(reqs, toks, cols)
    out.finish()


def tail(tokens, o1, s1, o2, s2, wo, gain, bias):
    reqs, toks, width = tokens.shape
    owners, planes = 16, 8
    dma = pltpu.SemaphoreType.DMA
    hbm = pl.BlockSpec(memory_space=pl.ANY)
    vmem = pl.BlockSpec(memory_space=pltpu.VMEM)
    bf16 = jnp.bfloat16
    wo = wo.reshape(planes, HD * owners // 2, width // planes)
    return pl.pallas_call(
        tail_kernel,
        out_shape=jax.ShapeDtypeStruct(tokens.shape, bf16),
        in_specs=[vmem, vmem, vmem, vmem, vmem, hbm, vmem, vmem],
        out_specs=vmem,
        scratch_shapes=[
            pltpu.VMEM(o2.shape, bf16),
            pltpu.VMEM(s2.shape, jnp.float32),
            pltpu.VMEM((owners, toks, HD), bf16),
            pltpu.VMEM((reqs, toks, HD * owners // 2), bf16),
            pltpu.VMEM(wo.shape, bf16),
            pltpu.VMEM((reqs * toks, width), jnp.float32),
            dma((2,)),
            dma((2,)),
            dma((owners,)),
            dma((owners,)),
            dma((planes,)),
        ],
        compiler_params=pltpu.CompilerParams(
            collective_id=1, has_side_effects=True, vmem_limit_bytes=40 << 20
        ),
        name="tail",
    )(tokens, o1, s1, o2, s2, wo, gain.reshape(1, width), bias.reshape(1, width))


def body(tokens, w_qkv, w_out, ln_gain, ln_bias, kv_pool, page_table, prefix_len, group_of):
    reqs, toks, width = tokens.shape
    owners = lax.axis_size("fsdp")
    rows = toks * owners
    q2, kv, pool, new_cache, wo = front(tokens, w_qkv, w_out, kv_pool)
    kv = kv.reshape(rows, 2 * HD)
    k, v = kv[:, :HD], kv[:, HD:]
    o1, s1, o2, s2 = attention(
        page_table, prefix_len, group_of, q2, k, v, pool
    )
    hidden = tail(tokens, o1, s1, o2, s2, wo, ln_gain, ln_bias)
    return hidden, new_cache


def solution(mesh):
    in_specs = (
        P("dp", "fsdp", None),
        P("fsdp", "dp"),
        P("fsdp", "dp"),
        P(),
        P(),
        P("fsdp", None, None),
        P(),
        P(),
        P("dp"),
    )
    out_specs = (P("dp", "fsdp", None), P("dp", "fsdp", None))
    return jax.shard_map(body, mesh=mesh, in_specs=in_specs, out_specs=out_specs, check_vma=False)
```

```python
import functools
import math

import jax
import jax.numpy as jnp
from jax import lax
from jax.experimental import pallas as pl
from jax.experimental.pallas import tpu as pltpu
from jax.sharding import PartitionSpec as P

HD = 128
NEG = -1e30
LN_EPS = 1e-06
LOG2E = 1.4426950408889634

NN = (((1,), (0,)), ((), ()))
NT = (((1,), (1,)), ((), ()))
TN = (((0,), (0,)), ((), ()))


def dot32(a, b, dims):
    return lax.dot_general(a, b, dims, preferred_element_type=jnp.float32)


def fold8(x, op):
    out = x[0:8]
    for i in range(1, x.shape[0] // 8):
        out = op(out, x[8 * i : 8 * i + 8])
    return out


def attention_kernel(
    half_slots,
    page_table,
    prefix_len,
    group_of,
    q_ref,
    kn_ref,
    vn_ref,
    pool_ref,
    o1_ref,
    s1_ref,
    o2_ref,
    s2_ref,
    sc,
    scn,
    m_ref,
    l_ref,
    acc,
    slot_list,
    base_list,
):
    f = lax.axis_index("fsdp")
    y, x = f // 8, lax.rem(f, 8) // 2
    rows = q_ref.shape[1]
    page = pool_ref.shape[1]
    n_pages = page_table.shape[1]
    inv_root = 1.0 / math.sqrt(HD)
    key_iota = lax.broadcasted_iota(jnp.int32, (page, rows), 0)
    for j in range(2):
        req = y if j == 0 else 1 - y
        group = group_of[req]
        length = prefix_len[group]

        def build(p, count):
            loc = page_table[group, p] - half_slots * y
            live = (loc >= 0) & (loc < half_slots) & (p * page < length)

            @pl.when(live)
            def _():
                slot_list[count] = lax.rem(loc, 4) * 8 + lax.rem(loc // 4 + 8 - 2 * x, 8)
                base_list[count] = p * page

            return count + live.astype(jnp.int32)

        count = lax.fori_loop(0, n_pages, build, jnp.int32(0))
        m_ref[...] = jnp.full(m_ref.shape, NEG, jnp.float32)
        l_ref[...] = jnp.zeros(l_ref.shape, jnp.float32)
        acc[...] = jnp.zeros(acc.shape, jnp.float32)
        q = q_ref[j]

        @pl.loop(0, count)
        def _(i):
            keys = pool_ref[slot_list[i], :, :HD]
            s = dot32(keys, q, NT) * inv_root
            s = jnp.where(key_iota < length - base_list[i], s, NEG)
            sc[i] = s
            m_ref[...] = jnp.maximum(m_ref[...], fold8(s, jnp.maximum))

        if j == 0:
            for kb in range(rows // page):
                lo = kb * page
                s = dot32(kn_ref[lo : lo + page, :], q[lo:, :], NT) * inv_root
                ki = lax.broadcasted_iota(jnp.int32, s.shape, 0)
                qi = lax.broadcasted_iota(jnp.int32, s.shape, 1)
                s = jnp.where(ki <= qi, s, NEG)
                scn[kb, :, lo:] = s
                m_ref[:, lo:] = jnp.maximum(m_ref[:, lo:], fold8(s, jnp.maximum))
        top = jnp.max(m_ref[...], axis=0, keepdims=True)

        @pl.loop(0, count)
        def _(i):
            e = jnp.exp2((sc[i] - top) * LOG2E)
            l_ref[...] += fold8(e, jnp.add)
            values = pool_ref[slot_list[i], :, HD:]
            acc[...] += dot32(values, e.astype(jnp.bfloat16), TN)

        if j == 0:
            for kb in range(rows // page):
                lo = kb * page
                e = jnp.exp2((scn[kb, :, lo:] - top[:, lo:]) * LOG2E)
                l_ref[:, lo:] += fold8(e, jnp.add)
                acc[:, lo:] += dot32(vn_ref[lo : lo + page, :], e.astype(jnp.bfloat16), TN)
        total = jnp.sum(l_ref[...], axis=0, keepdims=True)
        if j == 0:
            o1_ref[...] = acc[...]
            s1_ref[0:1, :] = top
            s1_ref[1:2, :] = total
            s1_ref[2:8, :] = jnp.zeros((6, rows), jnp.float32)
        else:
            o2_ref[...] = (acc[...] / jnp.maximum(total, 1.0)).astype(jnp.bfloat16)
            s2_ref[0:1, :] = top
            s2_ref[1:2, :] = total
            s2_ref[2:8, :] = jnp.zeros((6, rows), jnp.float32)


def attention(page_table, prefix_len, group_of, q2, k_new, v_new, pool):
    rows = q2.shape[1]
    slots, page = pool.shape[0], pool.shape[1]
    smem = pl.BlockSpec(memory_space=pltpu.SMEM)
    vmem = pl.BlockSpec(memory_space=pltpu.VMEM)
    return pl.pallas_call(
        functools.partial(attention_kernel, slots),
        out_shape=(
            jax.ShapeDtypeStruct((HD, rows), jnp.float32),
            jax.ShapeDtypeStruct((8, rows), jnp.float32),
            jax.ShapeDtypeStruct((HD, rows), jnp.bfloat16),
            jax.ShapeDtypeStruct((8, rows), jnp.float32),
        ),
        in_specs=[smem, smem, smem, vmem, vmem, vmem, vmem],
        out_specs=(vmem, vmem, vmem, vmem),
        scratch_shapes=[
            pltpu.VMEM((page_table.shape[1], page, rows), jnp.float32),
            pltpu.VMEM((rows // page, page, rows), jnp.float32),
            pltpu.VMEM((8, rows), jnp.float32),
            pltpu.VMEM((8, rows), jnp.float32),
            pltpu.VMEM((HD, rows), jnp.float32),
            pltpu.SMEM((page_table.shape[1],), jnp.int32),
            pltpu.SMEM((page_table.shape[1],), jnp.int32),
        ],
        compiler_params=pltpu.CompilerParams(vmem_limit_bytes=48 << 20),
        name="attend",
    )(page_table, prefix_len, group_of, q2, k_new, v_new, pool)


MESH = pl.DeviceIdType.MESH


class Copies:
    def __init__(self):
        self.started = []

    def send(self, src, dst, send_sem, recv_sem, device_id):
        copy = pltpu.make_async_remote_copy(
            src_ref=src,
            dst_ref=dst,
            send_sem=send_sem,
            recv_sem=recv_sem,
            device_id=device_id,
            device_id_type=MESH,
        )
        copy.start()
        self.started.append(copy)

    def finish(self):
        for copy in self.started:
            copy.wait_send()


def await_copy(dst, recv_sem):
    pltpu.make_async_copy(dst, dst, recv_sem).wait()


def front_kernel(
    tokens,
    w_ref,
    wo_ref,
    pool_in,
    q2,
    kv,
    pool,
    cache,
    wo,
    x_buf,
    wall,
    wh,
    x_send,
    x_recv,
    w1_send,
    w1_recv,
    w2_send,
    w2_recv,
    w3_send,
    w3_recv,
    p_send,
    p_recv,
    pz_send,
    pz_recv,
    c_send,
    c_recv,
    q_sem,
    local_sem,
    o1_send,
    o1_recv,
    o2_send,
    o2_recv,
):
    d = lax.axis_index("dp")
    f = lax.axis_index("fsdp")
    planes, owners = 8, 16
    heads = owners // 2
    y, h = f // heads, lax.rem(f, heads)
    x, core = h // 2, lax.rem(f, 2)
    toks = tokens.shape[1]
    wr = w_ref.shape[0]
    slots = pool_in.shape[0]

    def at(yy, xx, cc):
        return (yy * 4 + lax.rem(xx, 4)) * 2 + cc

    right, left = at(y, x + 1, core), at(y, x + 3, core)
    across, twin = at(1 - y, x, core), at(y, x, 1 - core)

    barrier = pltpu.get_barrier_semaphore()
    for k in range(1, owners):
        pl.semaphore_signal(
            barrier, inc=1, device_id={"fsdp": lax.rem(f + k, owners)}, device_id_type=MESH
        )
    for k in range(1, planes):
        pl.semaphore_signal(
            barrier, inc=1, device_id={"dp": lax.rem(d + k, planes)}, device_id_type=MESH
        )
    z, z_pair = d // 2, lax.rem(d, 2)
    other_plane = 2 * z + 1 - z_pair
    for k in range(1, owners):
        pl.semaphore_signal(
            barrier,
            inc=1,
            device_id={"dp": other_plane, "fsdp": lax.rem(f + k, owners)},
            device_id_type=MESH,
        )
    wq = w_ref.shape[0] // 4
    own_w = pltpu.make_async_copy(w_ref.at[pl.ds(wq * z, wq)], wall.at[d], local_sem.at[0])
    own_w.start()
    own_x = pltpu.make_async_copy(tokens.at[y], x_buf.at[f], local_sem.at[1])
    own_x.start()
    pl.semaphore_wait(barrier, 2 * owners + planes - 3)

    out = Copies()
    for k in range(1, planes):
        dest = lax.rem(d + k, planes)
        src = w_ref.at[pl.ds(pl.multiple_of(wq * (dest // 2), wq), wq)]
        out.send(src, wall.at[d], w1_send.at[k - 1], w1_recv.at[d], {"dp": dest})

    def send_x(n, src, who, dest):
        out.send(src, x_buf.at[who], x_send.at[n], x_recv.at[who], {"fsdp": dest})

    send_x(0, tokens.at[1 - y], f, across)
    send_x(1, tokens.at[y], f, right)
    send_x(2, tokens.at[y], f, left)
    send_x(3, tokens.at[y], f, twin)

    for s in range(planes):

        @pl.when(d == s)
        def _():
            own_w.wait()

        @pl.when(d != s)
        def _():
            await_copy(wall.at[s], w1_recv.at[s])

        for j in range(3):
            t, head = divmod(3 * s + j, heads)
            src = wall.at[s, :, pl.ds(HD * j, HD)]
            dst = wh.at[f, z, :, pl.ds(HD * t, HD)]

            @pl.when(h == head)
            def _():
                pltpu.make_async_copy(src, dst, w2_recv.at[h, t]).start()

            @pl.when(h != head)
            def _():
                pltpu.make_async_remote_copy(
                    src_ref=src,
                    dst_ref=dst,
                    send_sem=w2_send.at[3 * s + j],
                    recv_sem=w2_recv.at[h, t],
                    device_id={"fsdp": y * heads + head},
                    device_id_type=MESH,
                ).start()

    up = lax.rem(d + 2, planes)
    down = lax.rem(d + planes - 2, planes)

    def z_at(k):
        return lax.rem(z + k, 4)

    def wh_part(n, zz):
        row = y if n == 0 else 1 - y
        return wh.at[pl.ds(row * heads, heads), zz]

    def send_w(n, part, zz, dest):
        src = wh_part(part, zz)
        out.send(src, src, w3_send.at[n], w3_recv.at[zz, part], dest)

    for r in range(heads):
        for t in range(3):
            await_copy(wh.at[y * heads + r, z, :, pl.ds(HD * t, HD)], w2_recv.at[r, t])
    own_part = wh_part(0, z)
    out.send(own_part, own_part, w3_send.at[0], w3_recv.at[z, 1], {"fsdp": across})
    send_w(1, 0, z, {"dp": up})
    send_w(2, 0, z, {"dp": down})

    def pool_cols(t, head):
        return pl.ds(pl.multiple_of((t * heads + head) * HD, HD), HD)

    own_pool = []

    def send_pool():
        for t in range(2):
            cols = pl.ds(t * HD, HD)
            copy = pltpu.make_async_copy(
                pool_in.at[:, :, pool_cols(t, h)], pool.at[:, core, :, cols], local_sem.at[2 + t]
            )
            copy.start()
            own_pool.append(copy)
            out.send(
                pool_in.at[:, :, pool_cols(t, 2 * x + 1 - core)],
                pool.at[:, core, :, cols],
                p_send.at[0, t],
                p_recv.at[0, t],
                {"fsdp": twin},
            )
        for k in range(1, 4):
            for c in range(2):
                dest = at(y, x + k, c)
                place = 2 * (4 - k) + core
                for t in range(2):
                    out.send(
                        pool_in.at[z, :, pool_cols(t, lax.rem(dest, heads))],
                        pool.at[z, place, :, pl.ds(t * HD, HD)],
                        p_send.at[2 * k + c, t],
                        p_recv.at[place, t],
                        {"fsdp": dest},
                    )

    def pool_part(n, zz):
        return pool.at[zz, pl.ds(2 + 3 * n, 3)]

    def send_p(n, part, zz, dest):
        src = pool_part(part, zz)
        out.send(src, src, pz_send.at[n], pz_recv.at[zz, part], {"dp": dest})

    await_copy(x_buf.at[across], x_recv.at[across])
    send_x(4, x_buf.at[across], across, right)
    send_x(5, x_buf.at[across], across, left)
    send_x(6, x_buf.at[across], across, twin)
    a_left, b_left = at(y, x + 3, core), at(1 - y, x + 3, core)
    a_right, b_right = at(y, x + 1, core), at(1 - y, x + 1, core)
    a_far, b_far = at(y, x + 2, core), at(1 - y, x + 2, core)
    await_copy(x_buf.at[a_left], x_recv.at[a_left])
    send_x(7, x_buf.at[a_left], a_left, right)
    send_x(8, x_buf.at[a_left], a_left, twin)
    await_copy(x_buf.at[a_right], x_recv.at[a_right])
    send_x(9, x_buf.at[a_right], a_right, twin)

    await_copy(wh_part(1, z), w3_recv.at[z, 1])
    send_w(3, 1, z, {"dp": up})
    send_w(4, 1, z, {"dp": down})
    await_copy(wh_part(0, z_at(3)), w3_recv.at[z_at(3), 0])
    send_w(5, 0, z_at(3), {"dp": up})

    send_pool()

    await_copy(x_buf.at[b_right], x_recv.at[b_right])
    send_x(10, x_buf.at[b_right], b_right, left)
    send_x(11, x_buf.at[b_right], b_right, twin)
    await_copy(x_buf.at[b_left], x_recv.at[b_left])
    send_x(12, x_buf.at[b_left], b_left, twin)

    await_copy(wh_part(1, z_at(1)), w3_recv.at[z_at(1), 1])
    send_w(6, 1, z_at(1), {"dp": down})

    group = f // heads
    for p in range(2):
        for k in range(heads):
            dest = lax.rem(f // 2 + k, heads) * 2 + z_pair
            plane = d if p == 0 else other_plane
            sem = o1_send.at[p * heads + k]
            dst = wo.at[d, f]
            if p == 0 and k == 0:

                @pl.when(core == z_pair)
                def _():
                    pltpu.make_async_copy(wo_ref, dst, o1_recv.at[group]).start()

                @pl.when(core != z_pair)
                def _():
                    pltpu.make_async_remote_copy(
                        src_ref=wo_ref,
                        dst_ref=dst,
                        send_sem=sem,
                        recv_sem=o1_recv.at[group],
                        device_id={"fsdp": dest},
                        device_id_type=MESH,
                    ).start()

            else:
                out.send(wo_ref, dst, sem, o1_recv.at[group], {"dp": plane, "fsdp": dest})

    for place in range(2, 8):
        for t in range(2):
            await_copy(pool.at[z, place, :, pl.ds(t * HD, HD)], p_recv.at[place, t])
    for part in range(2):
        send_p(2 * part, part, z, up)
        send_p(2 * part + 1, part, z, down)

    await_copy(x_buf.at[a_far], x_recv.at[a_far])
    send_x(13, x_buf.at[a_far], a_far, twin)
    await_copy(x_buf.at[b_far], x_recv.at[b_far])
    send_x(14, x_buf.at[b_far], b_far, twin)
    for yy in range(2):
        for xx in range(4):
            who = at(yy, xx, 1 - core)
            await_copy(x_buf.at[who], x_recv.at[who])
    own_x.wait()
    for k, part in ((1, 0), (3, 1), (2, 0), (2, 1)):
        await_copy(wh_part(part, z_at(k)), w3_recv.at[z_at(k), part])

    @pl.loop(0, owners // 4)
    def _(i):
        left_rows = x_buf[pl.ds(4 * i, 4)].reshape(4 * toks, owners * wr)
        got = dot32(left_rows, wh[...].reshape(owners * wr, 3 * HD), NN).astype(jnp.bfloat16)
        q2[0, pl.ds(pl.multiple_of(4 * i * toks, 4 * toks), 4 * toks), :] = got[:, :HD]
        kv[pl.ds(4 * i, 4)] = got[:, HD:].reshape(4, toks, 2 * HD)

    out.send(q2.at[0], q2.at[1], q_sem.at[0], q_sem.at[1], {"fsdp": across})
    own_cache = []
    for k in range(owners):
        who = lax.rem(f + k, owners)
        for t in range(2):
            cols = pl.ds(pl.multiple_of((t * heads + h) * HD, HD), HD)
            src = kv.at[who, :, pl.ds(t * HD, HD)]
            dst = cache.at[y, :, cols]
            if k == 0:
                copy = pltpu.make_async_copy(src, dst, local_sem.at[4 + t])
                copy.start()
                own_cache.append(copy)
            else:
                out.send(src, dst, c_send.at[k, t], c_recv.at[f, t], {"fsdp": who})

    await_copy(pool_part(0, z_at(3)), pz_recv.at[z_at(3), 0])
    send_p(4, 0, z_at(3), up)
    await_copy(pool_part(1, z_at(1)), pz_recv.at[z_at(1), 1])
    send_p(5, 1, z_at(1), down)

    def half(plane, n):
        return wo.at[plane, pl.ds(n * heads, heads)]

    def send_o(n, plane, part, dp, ff):
        out.send(
            half(plane, part),
            half(plane, part),
            o2_send.at[n],
            o2_recv.at[plane, part],
            {"dp": dp, "fsdp": ff},
        )

    def z_plane(k, c):
        return 2 * z_at(k) + c

    for part in range(2):
        plane = z_plane(0, core)
        await_copy(half(plane, part), o1_recv.at[part])
        send_o(3 * part, plane, part, up, f)
        send_o(3 * part + 1, plane, part, down, f)
        send_o(3 * part + 2, plane, part, d, twin)
    for n, (k, part) in enumerate(((3, 0), (1, 1), (1, 0), (3, 1))):
        plane = z_plane(k, core)
        await_copy(half(plane, part), o2_recv.at[plane, part])
        if n == 0:
            send_o(6, plane, part, up, f)
        if n == 1:
            send_o(7, plane, part, down, f)
        send_o(8 + n, plane, part, d, twin)
    for part in range(2):
        plane = z_plane(2, core)
        await_copy(half(plane, part), o2_recv.at[plane, part])
        send_o(12 + part, plane, part, d, twin)
    for k in range(4):
        for part in range(2):
            plane = z_plane(k, 1 - core)
            await_copy(half(plane, part), o2_recv.at[plane, part])

    @pl.when(core != z_pair)
    def _():
        await_copy(wo.at[d, f], o1_send.at[0])

    await_copy(q2.at[1], q_sem.at[1])
    for copy in own_pool + own_cache:
        copy.wait()
    for t in range(2):
        await_copy(pool.at[:, 1 - core, :, pl.ds(t * HD, HD)], p_recv.at[0, t])
    for k, part in ((1, 0), (3, 1), (2, 0), (2, 1)):
        await_copy(pool_part(part, z_at(k)), pz_recv.at[z_at(k), part])
    for k in range(1, owners):
        who = lax.rem(f + k, owners)
        for t in range(2):
            cols = pl.ds(pl.multiple_of((t * heads + lax.rem(who, heads)) * HD, HD), HD)
            await_copy(cache.at[who // heads, :, cols], c_recv.at[who, t])
    for s in range(planes):
        for j in range(3):
            head = (3 * s + j) % heads

            @pl.when(h != head)
            def _():
                part = wall.at[s, :, pl.ds(HD * j, HD)]
                await_copy(part, w2_send.at[3 * s + j])

    out.finish()


def front(tokens, w_qkv, w_out, kv_pool):
    reqs, toks, width = tokens.shape
    slots, page, _ = kv_pool.shape
    owners, planes, heads = 16, 8, 8
    dma = pltpu.SemaphoreType.DMA
    hbm = pl.BlockSpec(memory_space=pltpu.HBM)
    vmem = pl.BlockSpec(memory_space=pltpu.VMEM)
    bf16 = jnp.bfloat16
    return pl.pallas_call(
        front_kernel,
        out_shape=(
            jax.ShapeDtypeStruct((2, owners * toks, HD), bf16),
            jax.ShapeDtypeStruct((owners, toks, 2 * HD), bf16),
            jax.ShapeDtypeStruct((slots, heads, page, 2 * HD), bf16),
            jax.ShapeDtypeStruct((reqs, toks, 2 * heads * HD), bf16),
            jax.ShapeDtypeStruct((planes, owners) + w_out.shape, bf16),
        ),
        in_specs=[hbm, hbm, hbm, hbm],
        out_specs=(vmem, vmem, hbm, hbm, hbm),
        scratch_shapes=[
            pltpu.VMEM((owners, toks, width), bf16),
            pltpu.VMEM((planes, w_qkv.shape[0] // 4, w_qkv.shape[1]), bf16),
            pltpu.VMEM((owners, 4, w_qkv.shape[0] // 4, 3 * HD), bf16),
            dma((15,)),
            dma((owners,)),
            dma((planes - 1,)),
            dma((planes,)),
            dma((3 * planes,)),
            dma((heads, 3)),
            dma((7,)),
            dma((4, 2)),
            dma((heads, 2)),
            dma((heads, 2)),
            dma((6,)),
            dma((4, 2)),
            dma((owners, 2)),
            dma((owners, 2)),
            dma((2,)),
            dma((6,)),
            dma((owners,)),
            dma((2,)),
            dma((15,)),
            dma((planes, 2)),
        ],
        compiler_params=pltpu.CompilerParams(
            collective_id=0, has_side_effects=True, vmem_limit_bytes=40 << 20
        ),
        name="front",
    )(tokens, w_qkv, w_out, kv_pool)


def tail_kernel(
    tokens,
    o1,
    s1,
    o2,
    s2,
    wo_hbm,
    gain,
    bias,
    hidden,
    o2_in,
    s2_in,
    at_out,
    at_in,
    wo,
    mixed,
    y_send,
    y_recv,
    a_send,
    a_recv,
    w_sem,
):
    f = lax.axis_index("fsdp")
    owners = 16
    heads = owners // 2
    y, h = f // heads, lax.rem(f, heads)
    across = (1 - y) * heads + h
    planes, depth, cols = wo.shape
    reqs, toks, width = tokens.shape
    rows = owners * toks

    barrier = pltpu.get_barrier_semaphore()
    for k in range(1, owners):
        pl.semaphore_signal(
            barrier, inc=1, device_id={"fsdp": lax.rem(f + k, owners)}, device_id_type=MESH
        )
    loads = []
    for p in range(planes):
        load = pltpu.make_async_copy(wo_hbm.at[p], wo.at[p], w_sem.at[p])
        load.start()
        loads.append(load)
    pl.semaphore_wait(barrier, owners - 1)
    out = Copies()
    out.send(s2, s2_in, y_send.at[0], y_recv.at[0], {"fsdp": across})
    out.send(o2, o2_in, y_send.at[1], y_recv.at[1], {"fsdp": across})
    await_copy(s2_in, y_recv.at[0])
    top = jnp.maximum(s1[0:1, :], s2_in[0:1, :])
    f1 = jnp.exp(s1[0:1, :] - top)
    f2 = jnp.exp(s2_in[0:1, :] - top) * s2_in[1:2, :]
    denom = s1[1:2, :] * f1 + f2
    await_copy(o2_in, y_recv.at[1])
    attn = (o1[...] * f1 + o2_in[...].astype(jnp.float32) * f2) / denom
    at_out[...] = attn.T.astype(jnp.bfloat16).reshape(owners, toks, HD)
    at_in[y, :, pl.ds(pl.multiple_of(h * HD, HD), HD)] = at_out[f]
    for k in range(1, owners):
        who = lax.rem(f + k, owners)
        dst = at_in.at[y, :, pl.ds(pl.multiple_of(h * HD, HD), HD)]
        out.send(at_out.at[who], dst, a_send.at[k], a_recv.at[f], {"fsdp": who})
    for k in range(1, owners):
        who = lax.rem(f + k, owners)
        col = pl.multiple_of(lax.rem(who, heads) * HD, HD)
        await_copy(at_in.at[who // heads, :, pl.ds(col, HD)], a_recv.at[who])
    left_rows = at_in[...].reshape(reqs * toks, depth)
    total = jnp.zeros((reqs * toks, 1), jnp.float32)
    for p in range(planes):
        loads[p].wait()
        part = dot32(left_rows, wo[p], NN)
        part = part + tokens[:, :, p * cols : (p + 1) * cols].reshape(
            reqs * toks, cols
        ).astype(jnp.float32)
        total = total + jnp.sum(part, axis=1, keepdims=True)
        mixed[:, p * cols : (p + 1) * cols] = part
    mean = total * (1.0 / width)
    square = jnp.zeros((reqs * toks, 1), jnp.float32)
    for p in range(planes):
        centred = mixed[:, p * cols : (p + 1) * cols] - mean
        square = square + jnp.sum(centred * centred, axis=1, keepdims=True)
    scale = lax.rsqrt(square * (1.0 / width) + LN_EPS)
    for p in range(planes):
        at = slice(p * cols, (p + 1) * cols)
        normed = (mixed[:, at] - mean) * scale * gain[0:1, at] + bias[0:1, at]
        hidden[:, :, at] = normed.astype(jnp.bfloat16).reshape(reqs, toks, cols)
    out.finish()


def tail(tokens, o1, s1, o2, s2, wo, gain, bias):
    reqs, toks, width = tokens.shape
    owners, planes = 16, 8
    dma = pltpu.SemaphoreType.DMA
    hbm = pl.BlockSpec(memory_space=pltpu.HBM)
    vmem = pl.BlockSpec(memory_space=pltpu.VMEM)
    bf16 = jnp.bfloat16
    wo = wo.reshape(planes, HD * owners // 2, width // planes)
    return pl.pallas_call(
        tail_kernel,
        out_shape=jax.ShapeDtypeStruct(tokens.shape, bf16),
        in_specs=[vmem, vmem, vmem, vmem, vmem, hbm, vmem, vmem],
        out_specs=vmem,
        scratch_shapes=[
            pltpu.VMEM(o2.shape, bf16),
            pltpu.VMEM(s2.shape, jnp.float32),
            pltpu.VMEM((owners, toks, HD), bf16),
            pltpu.VMEM((reqs, toks, HD * owners // 2), bf16),
            pltpu.VMEM(wo.shape, bf16),
            pltpu.VMEM((reqs * toks, width), jnp.float32),
            dma((2,)),
            dma((2,)),
            dma((owners,)),
            dma((owners,)),
            dma((planes,)),
        ],
        compiler_params=pltpu.CompilerParams(
            collective_id=1, has_side_effects=True, vmem_limit_bytes=40 << 20
        ),
        name="tail",
    )(tokens, o1, s1, o2, s2, wo, gain.reshape(1, width), bias.reshape(1, width))


def body(tokens, w_qkv, w_out, ln_gain, ln_bias, kv_pool, page_table, prefix_len, group_of):
    reqs, toks, width = tokens.shape
    owners = lax.axis_size("fsdp")
    rows = toks * owners
    q2, kv, pool, new_cache, wo = front(tokens, w_qkv, w_out, kv_pool)
    pool = pool.reshape((-1,) + pool.shape[2:])
    kv = kv.reshape(rows, 2 * HD)
    k, v = kv[:, :HD], kv[:, HD:]
    o1, s1, o2, s2 = attention(
        page_table, prefix_len, group_of, q2, k, v, pool
    )
    hidden = tail(tokens, o1, s1, o2, s2, wo, ln_gain, ln_bias)
    return hidden, new_cache


def solution(mesh):
    in_specs = (
        P("dp", "fsdp", None),
        P("fsdp", "dp"),
        P("fsdp", "dp"),
        P(),
        P(),
        P("fsdp", None, None),
        P(),
        P(),
        P("dp"),
    )
    out_specs = (P("dp", "fsdp", None), P("dp", "fsdp", None))
    return jax.shard_map(body, mesh=mesh, in_specs=in_specs, out_specs=out_specs, check_vma=False)
```

```python
import math

import jax
import jax.numpy as jnp
from jax import lax
from jax.experimental import pallas as pl
from jax.experimental.pallas import tpu as pltpu
from jax.sharding import PartitionSpec as P

HD = 128
NEG = -1e30
LN_EPS = 1e-06
LOG2E = 1.4426950408889634

NN = (((1,), (0,)), ((), ()))
NT = (((1,), (1,)), ((), ()))
TN = (((0,), (0,)), ((), ()))


def dot32(a, b, dims):
    return lax.dot_general(a, b, dims, preferred_element_type=jnp.float32)


def fold8(x, op):
    out = x[0:8]
    for i in range(1, x.shape[0] // 8):
        out = op(out, x[8 * i : 8 * i + 8])
    return out


MESH = pl.DeviceIdType.MESH


class Copies:
    def __init__(self):
        self.started = []

    def send(self, src, dst, send_sem, recv_sem, device_id):
        copy = pltpu.make_async_remote_copy(
            src_ref=src,
            dst_ref=dst,
            send_sem=send_sem,
            recv_sem=recv_sem,
            device_id=device_id,
            device_id_type=MESH,
        )
        copy.start()
        self.started.append(copy)

    def finish(self):
        for copy in self.started:
            copy.wait_send()


def await_copy(dst, recv_sem):
    pltpu.make_async_copy(dst, dst, recv_sem).wait()


def layer_kernel(
    page_table,
    prefix_len,
    group_of,
    tokens,
    w_ref,
    wo_ref,
    pool_in,
    gain,
    bias,
    hidden,
    cache,
    x_buf,
    wh,
    q2,
    kv,
    pool,
    wo,
    sc,
    scn,
    m_ref,
    l_ref,
    acc,
    o2,
    s2,
    o2_in,
    s2_in,
    at_out,
    at_in,
    mixed,
    tok,
    x_send,
    x_recv,
    w2_send,
    w2_recv,
    w3_send,
    w3_recv,
    p_send,
    p_recv,
    pz_send,
    pz_recv,
    c_send,
    c_recv,
    q_sem,
    local_sem,
    o1_send,
    o1_recv,
    o2_send,
    o2_recv,
    y_send,
    y_recv,
    a_send,
    a_recv,
):
    d = lax.axis_index("dp")
    f = lax.axis_index("fsdp")
    planes, owners = 8, 16
    heads = owners // 2
    y, h = f // heads, lax.rem(f, heads)
    x, core = h // 2, lax.rem(f, 2)
    z, z_pair = d // 2, lax.rem(d, 2)
    reqs, toks, width = tokens.shape
    rows = owners * toks
    slots, page, _ = pool_in.shape
    n_pages = page_table.shape[1]
    half_slots = heads * slots
    wq = w_ref.shape[0] // 4
    other_plane = 2 * z + 1 - z_pair
    up = lax.rem(d + 2, planes)
    down = lax.rem(d + planes - 2, planes)

    def at(yy, xx, cc):
        return (yy * 4 + lax.rem(xx, 4)) * 2 + cc

    def z_at(k):
        return lax.rem(z + k, 4)

    right, left = at(y, x + 1, core), at(y, x + 3, core)
    across, twin = at(1 - y, x, core), at(y, x, 1 - core)

    barrier = pltpu.get_barrier_semaphore()

    def greet(device_id):
        pl.semaphore_signal(barrier, inc=1, device_id=device_id, device_id_type=MESH)

    for k in range(1, owners):
        greet({"fsdp": lax.rem(f + k, owners)})
    for k in range(owners):
        greet({"dp": other_plane, "fsdp": lax.rem(f + k, owners)})
    greet({"dp": up})
    greet({"dp": down})
    for t in range(3):
        owner = (heads * t + h) // 3
        for r in range(heads):

            @pl.when((owner != d) | (h != r))
            def _():
                greet({"dp": owner, "fsdp": y * heads + r})

    holds_own = lax.rem(h + 3 * planes - 3 * d, heads) < 3
    own_x = pltpu.make_async_copy(tokens.at[y], x_buf.at[f], local_sem.at[1])
    own_x.start()
    own_tok = pltpu.make_async_copy(tokens, tok, local_sem.at[0])
    own_tok.start()
    pl.semaphore_wait(barrier, 2 * owners + 1 + 3 * planes - holds_own.astype(jnp.int32))

    out = Copies()
    w2_own = []
    for p in range(planes):
        plane = lax.rem(d + p, planes)
        zz = plane // 2
        for j in range(3):
            t, head = (3 * d + j) // heads, lax.rem(3 * d + j, heads)
            src = w_ref.at[pl.ds(pl.multiple_of(wq * zz, wq), wq), pl.ds(HD * j, HD)]
            dst = wh.at[f, zz, :, pl.ds(pl.multiple_of(HD * t, HD), HD)]
            if p:
                out.send(
                    src,
                    dst,
                    w2_send.at[p, j],
                    w2_recv.at[h, t],
                    {"dp": plane, "fsdp": y * heads + head},
                )
                continue

            @pl.when(head == h)
            def _():
                pltpu.make_async_copy(src, dst, w2_recv.at[h, t]).start()

            @pl.when(head != h)
            def _():
                pltpu.make_async_remote_copy(
                    src_ref=src,
                    dst_ref=dst,
                    send_sem=w2_send.at[0, j],
                    recv_sem=w2_recv.at[h, t],
                    device_id={"fsdp": y * heads + head},
                    device_id_type=MESH,
                ).start()

            w2_own.append((head, src, w2_send.at[0, j]))

    def send_x(n, src, who, dest):
        out.send(src, x_buf.at[who], x_send.at[n], x_recv.at[who], {"fsdp": dest})

    send_x(0, tokens.at[1 - y], f, across)
    send_x(1, tokens.at[y], f, right)
    send_x(2, tokens.at[y], f, left)
    send_x(3, tokens.at[y], f, twin)

    def pool_cols(t, head):
        return pl.ds(pl.multiple_of((t * heads + head) * HD, HD), HD)

    own_copies = []
    for t in range(2):
        cols = pl.ds(t * HD, HD)
        copy = pltpu.make_async_copy(
            pool_in.at[:, :, pool_cols(t, h)], pool.at[:, core, :, cols], local_sem.at[2 + t]
        )
        copy.start()
        own_copies.append(copy)
        out.send(
            pool_in.at[:, :, pool_cols(t, 2 * x + 1 - core)],
            pool.at[:, core, :, cols],
            p_send.at[0, t],
            p_recv.at[0, t],
            {"fsdp": twin},
        )
    for k in range(1, 4):
        for c in range(2):
            dest = at(y, x + k, c)
            place = 2 * (4 - k) + core
            for t in range(2):
                out.send(
                    pool_in.at[z, :, pool_cols(t, lax.rem(dest, heads))],
                    pool.at[z, place, :, pl.ds(t * HD, HD)],
                    p_send.at[2 * k + c, t],
                    p_recv.at[place, t],
                    {"fsdp": dest},
                )

    def wh_part(n, zz):
        row = y if n == 0 else 1 - y
        return wh.at[pl.ds(row * heads, heads), zz]

    def send_w(n, part, zz, dest):
        src = wh_part(part, zz)
        out.send(src, src, w3_send.at[n], w3_recv.at[zz, part], dest)

    for r in range(heads):
        for t in range(3):
            await_copy(wh.at[y * heads + r, z, :, pl.ds(HD * t, HD)], w2_recv.at[r, t])
    own_part = wh_part(0, z)
    out.send(own_part, own_part, w3_send.at[0], w3_recv.at[z, 1], {"fsdp": across})
    send_w(1, 0, z, {"dp": up})
    send_w(2, 0, z, {"dp": down})

    def pool_part(n, zz):
        return pool.at[zz, pl.ds(2 + 3 * n, 3)]

    def send_p(n, part, zz, dest):
        src = pool_part(part, zz)
        out.send(src, src, pz_send.at[n], pz_recv.at[zz, part], {"dp": dest})

    await_copy(x_buf.at[across], x_recv.at[across])
    send_x(4, x_buf.at[across], across, right)
    send_x(5, x_buf.at[across], across, left)
    send_x(6, x_buf.at[across], across, twin)
    a_left, b_left = at(y, x + 3, core), at(1 - y, x + 3, core)
    a_right, b_right = at(y, x + 1, core), at(1 - y, x + 1, core)
    a_far, b_far = at(y, x + 2, core), at(1 - y, x + 2, core)
    await_copy(x_buf.at[a_left], x_recv.at[a_left])
    send_x(7, x_buf.at[a_left], a_left, right)
    send_x(8, x_buf.at[a_left], a_left, twin)
    await_copy(x_buf.at[a_right], x_recv.at[a_right])
    send_x(9, x_buf.at[a_right], a_right, twin)
    await_copy(wh_part(1, z), w3_recv.at[z, 1])
    send_w(3, 1, z, {"dp": up})
    send_w(4, 1, z, {"dp": down})
    await_copy(wh_part(0, z_at(3)), w3_recv.at[z_at(3), 0])
    send_w(5, 0, z_at(3), {"dp": up})
    for place in range(2, 8):
        for t in range(2):
            await_copy(pool.at[z, place, :, pl.ds(t * HD, HD)], p_recv.at[place, t])
    for part in range(2):
        send_p(2 * part, part, z, up)
        send_p(2 * part + 1, part, z, down)
    await_copy(x_buf.at[b_right], x_recv.at[b_right])
    send_x(10, x_buf.at[b_right], b_right, left)
    send_x(11, x_buf.at[b_right], b_right, twin)
    await_copy(x_buf.at[b_left], x_recv.at[b_left])
    send_x(12, x_buf.at[b_left], b_left, twin)
    await_copy(wh_part(1, z_at(1)), w3_recv.at[z_at(1), 1])
    send_w(6, 1, z_at(1), {"dp": down})

    group = f // heads
    for p in range(2):
        for k in range(heads):
            dest = lax.rem(f // 2 + k, heads) * 2 + z_pair
            plane = d if p == 0 else other_plane
            sem = o1_send.at[p * heads + k]
            dst = wo.at[d, f]
            if p == 0 and k == 0:

                @pl.when(core == z_pair)
                def _():
                    pltpu.make_async_copy(wo_ref, dst, o1_recv.at[group]).start()

                @pl.when(core != z_pair)
                def _():
                    pltpu.make_async_remote_copy(
                        src_ref=wo_ref,
                        dst_ref=dst,
                        send_sem=sem,
                        recv_sem=o1_recv.at[group],
                        device_id={"fsdp": dest},
                        device_id_type=MESH,
                    ).start()

            else:
                out.send(wo_ref, dst, sem, o1_recv.at[group], {"dp": plane, "fsdp": dest})

    await_copy(pool_part(0, z_at(3)), pz_recv.at[z_at(3), 0])
    send_p(4, 0, z_at(3), up)
    await_copy(pool_part(1, z_at(1)), pz_recv.at[z_at(1), 1])
    send_p(5, 1, z_at(1), down)
    await_copy(x_buf.at[a_far], x_recv.at[a_far])
    send_x(13, x_buf.at[a_far], a_far, twin)
    await_copy(x_buf.at[b_far], x_recv.at[b_far])
    send_x(14, x_buf.at[b_far], b_far, twin)
    for yy in range(2):
        for xx in range(4):
            who = at(yy, xx, 1 - core)
            await_copy(x_buf.at[who], x_recv.at[who])
    own_x.wait()
    for k, part in ((1, 0), (3, 1), (2, 0), (2, 1)):
        await_copy(wh_part(part, z_at(k)), w3_recv.at[z_at(k), part])

    @pl.loop(0, owners // 4)
    def _(i):
        left_rows = x_buf[pl.ds(4 * i, 4)].reshape(4 * toks, width)
        got = dot32(left_rows, wh[...].reshape(width, 3 * HD), NN).astype(jnp.bfloat16)
        q2[0, pl.ds(pl.multiple_of(4 * i * toks, 4 * toks), 4 * toks), :] = got[:, :HD]
        kv[pl.ds(4 * i, 4)] = got[:, HD:].reshape(4, toks, 2 * HD)

    out.send(q2.at[0], q2.at[1], q_sem.at[0], q_sem.at[1], {"fsdp": across})

    def half(plane, n):
        return wo.at[plane, pl.ds(n * heads, heads)]

    def send_o(n, plane, part, dp, ff):
        src = half(plane, part)
        out.send(src, src, o2_send.at[n], o2_recv.at[plane, part], {"dp": dp, "fsdp": ff})

    def z_plane(k, c):
        return 2 * z_at(k) + c

    for part in range(2):
        plane = z_plane(0, core)
        await_copy(half(plane, part), o1_recv.at[part])
        send_o(3 * part, plane, part, up, f)
        send_o(3 * part + 1, plane, part, down, f)
        send_o(3 * part + 2, plane, part, d, twin)

    for k in range(owners):
        who = lax.rem(f + k, owners)
        for t in range(2):
            src = kv.at[who, :, pl.ds(t * HD, HD)]
            dst = cache.at[y, :, pool_cols(t, h)]
            if k == 0:
                copy = pltpu.make_async_copy(src, dst, local_sem.at[4 + t])
                copy.start()
                own_copies.append(copy)
            else:
                out.send(src, dst, c_send.at[k, t], c_recv.at[f, t], {"fsdp": who})

    for copy in own_copies[:2]:
        copy.wait()
    for t in range(2):
        await_copy(pool.at[:, 1 - core, :, pl.ds(t * HD, HD)], p_recv.at[0, t])
    for k, part in ((1, 0), (3, 1), (2, 0), (2, 1)):
        await_copy(pool_part(part, z_at(k)), pz_recv.at[z_at(k), part])

    inv_root = 1.0 / math.sqrt(HD)
    key_iota = lax.broadcasted_iota(jnp.int32, (page, rows), 0)

    def attend(j):
        req = y if j == 0 else 1 - y
        g = group_of[req]
        length = prefix_len[g]
        q = q2[j]

        def find(p):
            loc = page_table[g, p] - half_slots * y
            here = (loc >= 0) & (loc < half_slots)
            loc = jnp.clip(loc, 0, half_slots - 1)
            live = jnp.where(here, length - p * page, 0)
            return lax.rem(loc, slots), lax.rem(loc // slots + heads - 2 * x, heads), live

        m_ref[...] = jnp.full(m_ref.shape, NEG, jnp.float32)
        l_ref[...] = jnp.zeros(l_ref.shape, jnp.float32)
        acc[...] = jnp.zeros(acc.shape, jnp.float32)

        @pl.loop(0, n_pages)
        def _(p):
            a, b, live = find(p)
            s = dot32(pool[a, b, :, :HD], q, NT) * inv_root
            s = jnp.where(key_iota < live, s, NEG)
            sc[p] = s
            m_ref[...] = jnp.maximum(m_ref[...], fold8(s, jnp.maximum))

        if j == 0:
            for kb in range(rows // page):
                lo = kb * page
                keys = kv[2 * kb : 2 * kb + 2, :, :HD].reshape(page, HD)
                s = dot32(keys, q[lo:, :], NT) * inv_root
                ki = lax.broadcasted_iota(jnp.int32, s.shape, 0)
                qi = lax.broadcasted_iota(jnp.int32, s.shape, 1)
                s = jnp.where(ki <= qi, s, NEG)
                scn[kb, :, lo:] = s
                m_ref[:, lo:] = jnp.maximum(m_ref[:, lo:], fold8(s, jnp.maximum))
        top = jnp.maximum(jnp.max(m_ref[...], axis=0, keepdims=True), 0.5 * NEG)

        @pl.loop(0, n_pages // 2)
        def _(i):
            e = jnp.exp2((sc[pl.ds(2 * i, 2)].reshape(2 * page, rows) - top) * LOG2E)
            l_ref[...] += fold8(e, jnp.add)
            a, b, _ = find(2 * i)
            a1, b1, _ = find(2 * i + 1)
            values = jnp.concatenate([pool[a, b, :, HD:], pool[a1, b1, :, HD:]], 0)
            acc[...] += dot32(values, e.astype(jnp.bfloat16), TN)

        if j == 0:
            for kb in range(rows // page):
                lo = kb * page
                values = kv[2 * kb : 2 * kb + 2, :, HD:].reshape(page, HD)
                e = jnp.exp2((scn[kb, :, lo:] - top[:, lo:]) * LOG2E)
                l_ref[:, lo:] += fold8(e, jnp.add)
                acc[:, lo:] += dot32(values, e.astype(jnp.bfloat16), TN)
        return top, jnp.sum(l_ref[...], axis=0, keepdims=True)

    await_copy(q2.at[1], q_sem.at[1])
    top, total = attend(1)
    o2[...] = (acc[...] / jnp.maximum(total, 1.0)).astype(jnp.bfloat16)
    s2[0:1, :] = top
    s2[1:2, :] = total
    s2[2:8, :] = jnp.zeros((6, rows), jnp.float32)
    out.send(s2, s2_in, y_send.at[0], y_recv.at[0], {"fsdp": across})
    out.send(o2, o2_in, y_send.at[1], y_recv.at[1], {"fsdp": across})
    for n, (k, part) in enumerate(((3, 0), (1, 1), (1, 0), (3, 1))):
        plane = z_plane(k, core)
        await_copy(half(plane, part), o2_recv.at[plane, part])
        if n == 0:
            send_o(6, plane, part, up, f)
        if n == 1:
            send_o(7, plane, part, down, f)
        send_o(8 + n, plane, part, d, twin)

    top, total = attend(0)
    await_copy(s2_in, y_recv.at[0])
    await_copy(o2_in, y_recv.at[1])
    both = jnp.maximum(top, s2_in[0:1, :])
    f1 = jnp.exp(top - both)
    f2 = jnp.exp(s2_in[0:1, :] - both) * s2_in[1:2, :]
    attn = (acc[...] * f1 + o2_in[...].astype(jnp.float32) * f2) / (total * f1 + f2)
    at_out[...] = attn.T.astype(jnp.bfloat16).reshape(owners, toks, HD)
    at_in[y, :, pl.ds(pl.multiple_of(h * HD, HD), HD)] = at_out[f]
    for k in range(1, owners):
        who = lax.rem(f + k, owners)
        dst = at_in.at[y, :, pl.ds(pl.multiple_of(h * HD, HD), HD)]
        out.send(at_out.at[who], dst, a_send.at[k], a_recv.at[f], {"fsdp": who})
    for part in range(2):
        plane = z_plane(2, core)
        await_copy(half(plane, part), o2_recv.at[plane, part])
        send_o(12 + part, plane, part, d, twin)
    own_tok.wait()
    for k in range(1, owners):
        who = lax.rem(f + k, owners)
        col = pl.multiple_of(lax.rem(who, heads) * HD, HD)
        await_copy(at_in.at[who // heads, :, pl.ds(col, HD)], a_recv.at[who])
    for k in range(4):
        for part in range(2):
            plane = z_plane(k, 1 - core)
            await_copy(half(plane, part), o2_recv.at[plane, part])

    depth, cols = owners * wo.shape[2], wo.shape[3]
    left_rows = at_in[...].reshape(reqs * toks, depth)
    total = jnp.zeros((reqs * toks, 1), jnp.float32)
    for p in range(planes):
        part = dot32(left_rows, wo[p].reshape(depth, cols), NN)
        part = part + tok[:, :, p * cols : (p + 1) * cols].reshape(reqs * toks, cols).astype(
            jnp.float32
        )
        total = total + jnp.sum(part, axis=1, keepdims=True)
        mixed[:, p * cols : (p + 1) * cols] = part
    mean = total * (1.0 / width)
    square = jnp.zeros((reqs * toks, 1), jnp.float32)
    for p in range(planes):
        centred = mixed[:, p * cols : (p + 1) * cols] - mean
        square = square + jnp.sum(centred * centred, axis=1, keepdims=True)
    scale = lax.rsqrt(square * (1.0 / width) + LN_EPS)
    for p in range(planes):
        span = slice(p * cols, (p + 1) * cols)
        normed = (mixed[:, span] - mean) * scale * gain[0:1, span] + bias[0:1, span]
        hidden[:, :, span] = normed.astype(jnp.bfloat16).reshape(reqs, toks, cols)

    for copy in own_copies[2:]:
        copy.wait()
    for k in range(1, owners):
        who = lax.rem(f + k, owners)
        for t in range(2):
            await_copy(cache.at[who // heads, :, pool_cols(t, lax.rem(who, heads))], c_recv.at[who, t])

    @pl.when(core != z_pair)
    def _():
        await_copy(wo.at[d, f], o1_send.at[0])

    for head, src, sem in w2_own:

        @pl.when(head != h)
        def _():
            await_copy(src, sem)

    out.finish()


def body(tokens, w_qkv, w_out, ln_gain, ln_bias, kv_pool, page_table, prefix_len, group_of):
    reqs, toks, width = tokens.shape
    slots, page, _ = kv_pool.shape
    owners, planes, heads = 16, 8, 8
    rows = owners * toks
    dma = pltpu.SemaphoreType.DMA
    hbm = pl.BlockSpec(memory_space=pltpu.HBM)
    vmem = pl.BlockSpec(memory_space=pltpu.VMEM)
    smem = pl.BlockSpec(memory_space=pltpu.SMEM)
    bf16, f32 = jnp.bfloat16, jnp.float32
    return pl.pallas_call(
        layer_kernel,
        out_shape=(
            jax.ShapeDtypeStruct(tokens.shape, bf16),
            jax.ShapeDtypeStruct((reqs, toks, 2 * heads * HD), bf16),
        ),
        in_specs=[smem, smem, smem, hbm, hbm, hbm, hbm, vmem, vmem],
        out_specs=(vmem, hbm),
        scratch_shapes=[
            pltpu.VMEM((owners, toks, width), bf16),
            pltpu.VMEM((owners, 4, w_qkv.shape[0] // 4, 3 * HD), bf16),
            pltpu.VMEM((2, rows, HD), bf16),
            pltpu.VMEM((owners, toks, 2 * HD), bf16),
            pltpu.VMEM((slots, heads, page, 2 * HD), bf16),
            pltpu.VMEM((planes, owners) + w_out.shape, bf16),
            pltpu.VMEM((page_table.shape[1], page, rows), f32),
            pltpu.VMEM((rows // page, page, rows), f32),
            pltpu.VMEM((8, rows), f32),
            pltpu.VMEM((8, rows), f32),
            pltpu.VMEM((HD, rows), f32),
            pltpu.VMEM((HD, rows), bf16),
            pltpu.VMEM((8, rows), f32),
            pltpu.VMEM((HD, rows), bf16),
            pltpu.VMEM((8, rows), f32),
            pltpu.VMEM((owners, toks, HD), bf16),
            pltpu.VMEM((reqs, toks, heads * HD), bf16),
            pltpu.VMEM((reqs * toks, width), f32),
            pltpu.VMEM(tokens.shape, bf16),
            dma((15,)),
            dma((owners,)),
            dma((planes, 3)),
            dma((heads, 3)),
            dma((7,)),
            dma((4, 2)),
            dma((heads, 2)),
            dma((heads, 2)),
            dma((6,)),
            dma((4, 2)),
            dma((owners, 2)),
            dma((owners, 2)),
            dma((2,)),
            dma((6,)),
            dma((owners,)),
            dma((2,)),
            dma((15,)),
            dma((planes, 2)),
            dma((2,)),
            dma((2,)),
            dma((owners,)),
            dma((owners,)),
        ],
        compiler_params=pltpu.CompilerParams(
            collective_id=0, has_side_effects=True, vmem_limit_bytes=67043328
        ),
        name="layer",
    )(
        page_table,
        prefix_len,
        group_of,
        tokens,
        w_qkv,
        w_out,
        kv_pool,
        ln_gain.reshape(1, width),
        ln_bias.reshape(1, width),
    )


def solution(mesh):
    in_specs = (
        P("dp", "fsdp", None),
        P("fsdp", "dp"),
        P("fsdp", "dp"),
        P(),
        P(),
        P("fsdp", None, None),
        P(),
        P(),
        P("dp"),
    )
    out_specs = (P("dp", "fsdp", None), P("dp", "fsdp", None))
    return jax.shard_map(body, mesh=mesh, in_specs=in_specs, out_specs=out_specs, check_vma=False)
```

```python
import math

import jax
import jax.numpy as jnp
from jax import lax
from jax.experimental import pallas as pl
from jax.experimental.pallas import tpu as pltpu
from jax.sharding import PartitionSpec as P

HD = 128
NEG = -1e30
LN_EPS = 1e-06
LOG2E = 1.4426950408889634

NN = (((1,), (0,)), ((), ()))
NT = (((1,), (1,)), ((), ()))
TN = (((0,), (0,)), ((), ()))


def dot32(a, b, dims):
    return lax.dot_general(a, b, dims, preferred_element_type=jnp.float32)


def fold8(x, op):
    out = x[0:8]
    for i in range(1, x.shape[0] // 8):
        out = op(out, x[8 * i : 8 * i + 8])
    return out


MESH = pl.DeviceIdType.MESH


class Copies:
    def __init__(self):
        self.started = []

    def send(self, src, dst, send_sem, recv_sem, device_id):
        copy = pltpu.make_async_remote_copy(
            src_ref=src,
            dst_ref=dst,
            send_sem=send_sem,
            recv_sem=recv_sem,
            device_id=device_id,
            device_id_type=MESH,
        )
        copy.start()
        self.started.append(copy)

    def finish(self):
        for copy in self.started:
            copy.wait_send()


def await_copy(dst, recv_sem):
    pltpu.make_async_copy(dst, dst, recv_sem).wait()


def layer_kernel(
    page_table,
    prefix_len,
    group_of,
    tokens,
    w_ref,
    wo_ref,
    pool_in,
    gain,
    bias,
    hidden,
    cache,
    x_buf,
    wh,
    q2,
    kv,
    pool,
    wo,
    wo_both,
    sc,
    scn,
    m_ref,
    l_ref,
    acc,
    m_other,
    l_other,
    acc_other,
    o2,
    s2,
    o2_in,
    s2_in,
    at_out,
    at_in,
    mixed,
    tok,
    x_send,
    x_recv,
    w2_send,
    w2_recv,
    w3_send,
    w3_recv,
    p_send,
    p_recv,
    pz_send,
    pz_recv,
    c_send,
    c_recv,
    q_send,
    q_recv,
    local_sem,
    o0_send,
    o0_recv,
    o1_send,
    o1_recv,
    o2_send,
    o2_recv,
    y_send,
    y_recv,
    a_send,
    a_recv,
):
    d = lax.axis_index("dp")
    f = lax.axis_index("fsdp")
    planes, owners = 8, 16
    heads = owners // 2
    y, h = f // heads, lax.rem(f, heads)
    x, core = h // 2, lax.rem(f, 2)
    z, z_pair = d // 2, lax.rem(d, 2)
    reqs, toks, width = tokens.shape
    rows = owners * toks
    slots, page, _ = pool_in.shape
    n_pages = page_table.shape[1]
    half_slots = heads * slots
    wq = w_ref.shape[0] // 4
    other_plane = 2 * z + 1 - z_pair
    up = lax.rem(d + 2, planes)
    down = lax.rem(d + planes - 2, planes)

    def at(yy, xx, cc):
        return (yy * 4 + lax.rem(xx, 4)) * 2 + cc

    def z_at(k):
        return lax.rem(z + k, 4)

    right, left = at(y, x + 1, core), at(y, x + 3, core)
    across, twin = at(1 - y, x, core), at(y, x, 1 - core)

    barrier = pltpu.get_barrier_semaphore()

    def greet(device_id):
        pl.semaphore_signal(barrier, inc=1, device_id=device_id, device_id_type=MESH)

    for k in range(1, owners):
        greet({"fsdp": lax.rem(f + k, owners)})
    greet({"dp": other_plane})
    greet({"dp": up})
    greet({"dp": down})
    for t in range(3):
        owner = (heads * t + h) // 3
        for r in range(heads):

            @pl.when((owner != d) | (h != r))
            def _():
                greet({"dp": owner, "fsdp": y * heads + r})

    holds_own = lax.rem(h + 3 * planes - 3 * d, heads) < 3
    own_x = pltpu.make_async_copy(tokens.at[y], x_buf.at[f], local_sem.at[1])
    own_x.start()
    own_tok = pltpu.make_async_copy(tokens, tok, local_sem.at[0])
    own_tok.start()
    own_wo = pltpu.make_async_copy(wo_ref, wo_both.at[z_pair], local_sem.at[6])
    own_wo.start()
    pl.semaphore_wait(barrier, owners + 2 + 3 * planes - holds_own.astype(jnp.int32))

    out = Copies()
    w2_own = []
    for p in range(planes):
        plane = lax.rem(d + p, planes)
        zz = plane // 2
        for j in range(3):
            t, head = (3 * d + j) // heads, lax.rem(3 * d + j, heads)
            src = w_ref.at[pl.ds(pl.multiple_of(wq * zz, wq), wq), pl.ds(HD * j, HD)]
            dst = wh.at[f, zz, :, pl.ds(pl.multiple_of(HD * t, HD), HD)]
            if p:
                out.send(
                    src,
                    dst,
                    w2_send.at[p, j],
                    w2_recv.at[h, t],
                    {"dp": plane, "fsdp": y * heads + head},
                )
                continue

            @pl.when(head == h)
            def _():
                pltpu.make_async_copy(src, dst, w2_recv.at[h, t]).start()

            @pl.when(head != h)
            def _():
                pltpu.make_async_remote_copy(
                    src_ref=src,
                    dst_ref=dst,
                    send_sem=w2_send.at[0, j],
                    recv_sem=w2_recv.at[h, t],
                    device_id={"fsdp": y * heads + head},
                    device_id_type=MESH,
                ).start()

            w2_own.append((head, src, w2_send.at[0, j]))

    half_toks = toks // 2

    def send_x(n, src, who, part, dest):
        dst = x_buf.at[who, pl.ds(part * half_toks, half_toks)]
        out.send(
            dst if src is None else src.at[pl.ds(part * half_toks, half_toks)],
            dst,
            x_send.at[n, part],
            x_recv.at[who, part],
            {"fsdp": dest},
        )

    def await_x(who, part):
        await_copy(x_buf.at[who, pl.ds(part * half_toks, half_toks)], x_recv.at[who, part])

    for part in range(2):
        send_x(0, tokens.at[1 - y], f, part, across)
        send_x(1, tokens.at[y], f, part, right)
        send_x(2, tokens.at[y], f, part, left)
        send_x(3, tokens.at[y], f, part, twin)

    def pool_cols(t, head):
        return pl.ds(pl.multiple_of((t * heads + head) * HD, HD), HD)

    own_copies = []
    for t in range(2):
        cols = pl.ds(t * HD, HD)
        copy = pltpu.make_async_copy(
            pool_in.at[:, :, pool_cols(t, h)], pool.at[:, core, :, cols], local_sem.at[2 + t]
        )
        copy.start()
        own_copies.append(copy)
        out.send(
            pool_in.at[:, :, pool_cols(t, 2 * x + 1 - core)],
            pool.at[:, core, :, cols],
            p_send.at[0, t],
            p_recv.at[0, t],
            {"fsdp": twin},
        )
    for k in range(1, 4):
        for c in range(2):
            dest = at(y, x + k, c)
            place = 2 * (4 - k) + core
            for t in range(2):
                out.send(
                    pool_in.at[z, :, pool_cols(t, lax.rem(dest, heads))],
                    pool.at[z, place, :, pl.ds(t * HD, HD)],
                    p_send.at[2 * k + c, t],
                    p_recv.at[place, t],
                    {"fsdp": dest},
                )

    def wh_part(n, zz):
        row = y if n == 0 else 1 - y
        return wh.at[pl.ds(row * heads, heads), zz]

    def send_w(n, part, zz, dest):
        src = wh_part(part, zz)
        out.send(src, src, w3_send.at[n], w3_recv.at[zz, part], dest)

    for r in range(heads):
        for t in range(3):
            await_copy(wh.at[y * heads + r, z, :, pl.ds(HD * t, HD)], w2_recv.at[r, t])
    own_part = wh_part(0, z)
    out.send(own_part, own_part, w3_send.at[0], w3_recv.at[z, 1], {"fsdp": across})
    send_w(1, 0, z, {"dp": up})
    send_w(2, 0, z, {"dp": down})

    def pool_part(n, zz):
        return pool.at[zz, pl.ds(2 + 3 * n, 3)]

    def send_p(n, part, zz, dest):
        src = pool_part(part, zz)
        out.send(src, src, pz_send.at[n], pz_recv.at[zz, part], {"dp": dest})

    a_left, b_left = at(y, x + 3, core), at(1 - y, x + 3, core)
    a_right, b_right = at(y, x + 1, core), at(1 - y, x + 1, core)
    a_far, b_far = at(y, x + 2, core), at(1 - y, x + 2, core)
    for part in range(2):
        await_x(across, part)
        send_x(4, None, across, part, right)
        send_x(5, None, across, part, left)
        send_x(6, None, across, part, twin)
    for part in range(2):
        await_x(a_left, part)
        send_x(7, None, a_left, part, right)
        send_x(8, None, a_left, part, twin)
        await_x(a_right, part)
        send_x(9, None, a_right, part, twin)
    await_copy(wh_part(0, z_at(3)), w3_recv.at[z_at(3), 0])
    send_w(5, 0, z_at(3), {"dp": up})
    await_copy(wh_part(1, z), w3_recv.at[z, 1])
    send_w(3, 1, z, {"dp": up})
    send_w(4, 1, z, {"dp": down})
    out.send(wo_ref, wo_both.at[z_pair], o0_send, o0_recv, {"dp": other_plane})
    for place in range(2, 8):
        for t in range(2):
            await_copy(pool.at[z, place, :, pl.ds(t * HD, HD)], p_recv.at[place, t])
    send_p(0, 0, z, up)
    send_p(1, 1, z, up)
    for part in range(2):
        await_x(b_right, part)
        send_x(10, None, b_right, part, left)
        send_x(11, None, b_right, part, twin)
        await_x(b_left, part)
        send_x(12, None, b_left, part, twin)
    await_copy(wh_part(1, z_at(1)), w3_recv.at[z_at(1), 1])
    send_w(6, 1, z_at(1), {"dp": down})
    send_p(2, 1, z, down)
    send_p(3, 0, z, down)

    group = f // heads
    own_wo.wait()
    await_copy(wo_both.at[1 - z_pair], o0_recv)
    pltpu.make_async_copy(wo_both.at[core], wo.at[2 * z + core, f], o1_recv.at[group]).start()
    for k in range(1, owners):
        dest = lax.rem(f + k, owners)
        c = lax.rem(dest, 2)
        out.send(
            wo_both.at[c], wo.at[2 * z + c, f], o1_send.at[k], o1_recv.at[group], {"fsdp": dest}
        )

    await_copy(pool_part(0, z_at(3)), pz_recv.at[z_at(3), 0])
    send_p(4, 0, z_at(3), up)
    await_copy(pool_part(1, z_at(1)), pz_recv.at[z_at(1), 1])
    send_p(5, 1, z_at(1), down)
    for part in range(2):
        await_x(a_far, part)
        send_x(13, None, a_far, part, twin)
    for k, part in ((1, 0), (3, 1), (2, 0), (2, 1)):
        await_copy(wh_part(part, z_at(k)), w3_recv.at[z_at(k), part])
    for part in range(2):
        await_x(b_far, part)
        send_x(14, None, b_far, part, twin)
    own_x.wait()

    span = rows // 2
    for k in range(2):
        row = y if k == 0 else 1 - y
        for xx in range(4):
            for part in range(2):
                await_x(at(row, xx, 1 - core), part)

        @pl.loop(0, 2)
        def _(i):
            first = row * heads + 4 * i
            left_rows = x_buf[pl.ds(first, 4)].reshape(4 * toks, width)
            got = dot32(left_rows, wh[...].reshape(width, 3 * HD), NN).astype(jnp.bfloat16)
            q2[0, pl.ds(pl.multiple_of(first * toks, 4 * toks), 4 * toks), :] = got[:, :HD]
            kv[pl.ds(first, 4)] = got[:, HD:].reshape(4, toks, 2 * HD)

        at_rows = pl.ds(pl.multiple_of(row * span, span), span)
        out.send(
            q2.at[0, at_rows], q2.at[1, at_rows], q_send.at[k], q_recv.at[k], {"fsdp": across}
        )

    def half(plane, n):
        return wo.at[plane, pl.ds(n * heads, heads)]

    def send_o(n, plane, part, dp, ff):
        src = half(plane, part)
        out.send(src, src, o2_send.at[n], o2_recv.at[plane, part], {"dp": dp, "fsdp": ff})

    def z_plane(k, c):
        return 2 * z_at(k) + c

    plane = z_plane(0, core)
    for part in range(2):
        await_copy(half(plane, part), o1_recv.at[part])
    send_o(0, plane, 0, up, f)
    send_o(1, plane, 1, down, f)
    send_o(2, plane, 1, up, f)
    send_o(3, plane, 0, down, f)
    for part in range(2):
        send_o(4 + part, plane, part, d, twin)

    inv_root = 1.0 / math.sqrt(HD)
    key_iota = lax.broadcasted_iota(jnp.int32, (page, span), 0)
    query_iota = lax.broadcasted_iota(jnp.int32, (page, span), 1)

    def put(index, scores, live, m_at):
        for n in range(2):
            part = jnp.where(live[n], scores[n * page : (n + 1) * page], NEG)
            m_at[...] = jnp.maximum(m_at[...], fold8(part, jnp.maximum))
            index(n)[...] = part

    def add(scores, values, top, l_at, acc_at):
        e = jnp.exp2((scores.reshape(2 * page, span) - top) * LOG2E)
        l_at[...] += fold8(e, jnp.add)
        acc_at[...] += dot32(values, e.astype(jnp.bfloat16), TN)

    def highest(m_at):
        return jnp.maximum(jnp.max(m_at[...], axis=0, keepdims=True), 0.5 * NEG)

    def pages(j, hh):
        g = group_of[y if j == 0 else 1 - y]
        length = prefix_len[g]

        def find(p):
            loc = page_table[g, p] - half_slots * y
            here = (loc >= 0) & (loc < half_slots)
            loc = jnp.clip(loc, 0, half_slots - 1)
            live = jnp.where(here, length - p * page, 0)
            return lax.rem(loc, slots), lax.rem(loc // slots + heads - 2 * x, heads), live

        def both(i, cols):
            a, b, live_a = find(2 * i)
            c, e, live_b = find(2 * i + 1)
            return jnp.concatenate([pool[a, b, :, cols], pool[c, e, :, cols]], 0), (live_a, live_b)

        def scores(q, m_at):
            @pl.loop(0, n_pages // 2)
            def _(i):
                keys, live = both(i, slice(0, HD))
                put(
                    lambda n: sc.at[2 * i + n],
                    dot32(keys, q, NT) * inv_root,
                    [key_iota < live[0], key_iota < live[1]],
                    m_at,
                )

        def sums(top, l_at, acc_at):
            @pl.loop(0, n_pages // 2)
            def _(i):
                values, _ = both(i, slice(HD, 2 * HD))
                add(sc[pl.ds(2 * i, 2)], values, top, l_at, acc_at)

        return scores, sums

    def queries(j, hh):
        return q2[j, pl.ds(pl.multiple_of(hh * span, span), span), :]

    m_ref[...] = jnp.full(m_ref.shape, NEG, jnp.float32)
    l_ref[...] = jnp.zeros(l_ref.shape, jnp.float32)
    acc[...] = jnp.zeros(acc.shape, jnp.float32)
    pairs = span // (2 * page)
    for hh in range(2):
        q = queries(0, hh)

        @pl.loop(0, pairs * (hh + 1))
        def _(i):
            keys = kv[pl.ds(4 * i, 4), :, :HD].reshape(2 * page, HD)
            ahead = [
                key_iota + (2 * i + n) * page <= query_iota + hh * span for n in range(2)
            ]
            put(
                lambda n: scn.at[hh, 2 * i + n], dot32(keys, q, NT) * inv_root, ahead, m_ref.at[hh]
            )

    for copy in own_copies:
        copy.wait()
    for t in range(2):
        await_copy(pool.at[:, 1 - core, :, pl.ds(t * HD, HD)], p_recv.at[0, t])
    for k, part in ((1, 0), (3, 1), (2, 0), (2, 1)):
        await_copy(pool_part(part, z_at(k)), pz_recv.at[z_at(k), part])

    for k in range(2):
        hh = 1 - y if k == 0 else y
        await_copy(q2.at[1, pl.ds(pl.multiple_of(hh * span, span), span)], q_recv.at[k])
        q = queries(1, hh)
        scores, sums = pages(1, hh)
        m_other[...] = jnp.full(m_other.shape, NEG, jnp.float32)
        l_other[...] = jnp.zeros(l_other.shape, jnp.float32)
        acc_other[...] = jnp.zeros(acc_other.shape, jnp.float32)
        scores(q, m_other)
        top = highest(m_other)
        sums(top, l_other, acc_other)
        total = jnp.sum(l_other[...], axis=0, keepdims=True)
        o2[k] = (acc_other[...] / jnp.maximum(total, 1.0)).astype(jnp.bfloat16)
        s2[k, 0:1, :] = top
        s2[k, 1:2, :] = total
        s2[k, 2:8, :] = jnp.zeros((6, span), jnp.float32)
        out.send(s2.at[k], s2_in.at[k], y_send.at[0, k], y_recv.at[0, k], {"fsdp": across})
        out.send(o2.at[k], o2_in.at[k], y_send.at[1, k], y_recv.at[1, k], {"fsdp": across})

    own_cache = []
    for k in range(owners):
        who = lax.rem(f + k, owners)
        for t in range(2):
            src = kv.at[who, :, pl.ds(t * HD, HD)]
            dst = cache.at[y, :, pool_cols(t, h)]
            if k == 0:
                copy = pltpu.make_async_copy(src, dst, local_sem.at[4 + t])
                copy.start()
                own_cache.append(copy)
            else:
                out.send(src, dst, c_send.at[k, t], c_recv.at[f, t], {"fsdp": who})

    for n, (k, part) in enumerate(((3, 0), (1, 1))):
        plane = z_plane(k, core)
        await_copy(half(plane, part), o2_recv.at[plane, part])
        send_o(6 + n, plane, part, down if n else up, f)
        send_o(8 + n, plane, part, d, twin)

    for k in range(2):
        hh = y if k == 0 else 1 - y
        q = queries(0, hh)
        scores, sums = pages(0, hh)
        scores(q, m_ref.at[hh])
        top = highest(m_ref.at[hh])
        sums(top, l_ref.at[hh], acc.at[hh])

        @pl.loop(0, pairs * (hh + 1))
        def _(i):
            values = kv[pl.ds(4 * i, 4), :, HD:].reshape(2 * page, HD)
            add(scn[hh, pl.ds(2 * i, 2)], values, top, l_ref.at[hh], acc.at[hh])

        total = jnp.sum(l_ref[hh], axis=0, keepdims=True)
        await_copy(s2_in.at[k], y_recv.at[0, k])
        await_copy(o2_in.at[k], y_recv.at[1, k])
        both_top = jnp.maximum(top, s2_in[k, 0:1, :])
        f1 = jnp.exp(top - both_top)
        f2 = jnp.exp(s2_in[k, 0:1, :] - both_top) * s2_in[k, 1:2, :]
        attn = (acc[hh] * f1 + o2_in[k].astype(jnp.float32) * f2) / (total * f1 + f2)
        at_out[pl.ds(hh * heads, heads)] = attn.T.astype(jnp.bfloat16).reshape(heads, toks, HD)
        col = pl.ds(pl.multiple_of(h * HD, HD), HD)
        if k == 0:
            at_in[y, :, col] = at_out[f]
        for i in range(1 - k, heads):
            who = hh * heads + lax.rem(h + i, heads)
            n = k * heads + i
            out.send(at_out.at[who], at_in.at[y, :, col], a_send.at[n], a_recv.at[f], {"fsdp": who})
        if k == 0:
            for n, (kk, part) in enumerate(((1, 0), (3, 1))):
                plane = z_plane(kk, core)
                await_copy(half(plane, part), o2_recv.at[plane, part])
                send_o(10 + n, plane, part, d, twin)
    for part in range(2):
        plane = z_plane(2, core)
        await_copy(half(plane, part), o2_recv.at[plane, part])
        send_o(12 + part, plane, part, d, twin)
    own_tok.wait()
    for k in range(1, owners):
        who = lax.rem(f + k, owners)
        col = pl.multiple_of(lax.rem(who, heads) * HD, HD)
        await_copy(at_in.at[who // heads, :, pl.ds(col, HD)], a_recv.at[who])
    for k in range(4):
        for part in range(2):
            plane = z_plane(k, 1 - core)
            await_copy(half(plane, part), o2_recv.at[plane, part])

    depth, cols = owners * wo.shape[2], wo.shape[3]
    left_rows = at_in[...].reshape(reqs * toks, depth)
    total = jnp.zeros((reqs * toks, 1), jnp.float32)
    for p in range(planes):
        part = dot32(left_rows, wo[p].reshape(depth, cols), NN)
        part = part + tok[:, :, p * cols : (p + 1) * cols].reshape(reqs * toks, cols).astype(
            jnp.float32
        )
        total = total + jnp.sum(part, axis=1, keepdims=True)
        mixed[:, p * cols : (p + 1) * cols] = part
    mean = total * (1.0 / width)
    square = jnp.zeros((reqs * toks, 1), jnp.float32)
    for p in range(planes):
        centred = mixed[:, p * cols : (p + 1) * cols] - mean
        square = square + jnp.sum(centred * centred, axis=1, keepdims=True)
    scale = lax.rsqrt(square * (1.0 / width) + LN_EPS)
    for p in range(planes):
        span = slice(p * cols, (p + 1) * cols)
        normed = (mixed[:, span] - mean) * scale * gain[0:1, span] + bias[0:1, span]
        hidden[:, :, span] = normed.astype(jnp.bfloat16).reshape(reqs, toks, cols)

    for copy in own_cache:
        copy.wait()
    for k in range(1, owners):
        who = lax.rem(f + k, owners)
        for t in range(2):
            await_copy(cache.at[who // heads, :, pool_cols(t, lax.rem(who, heads))], c_recv.at[who, t])

    for head, src, sem in w2_own:

        @pl.when(head != h)
        def _():
            await_copy(src, sem)

    out.finish()


def body(tokens, w_qkv, w_out, ln_gain, ln_bias, kv_pool, page_table, prefix_len, group_of):
    reqs, toks, width = tokens.shape
    slots, page, _ = kv_pool.shape
    owners, planes, heads = 16, 8, 8
    rows = owners * toks
    dma = pltpu.SemaphoreType.DMA
    hbm = pl.BlockSpec(memory_space=pltpu.HBM)
    vmem = pl.BlockSpec(memory_space=pltpu.VMEM)
    smem = pl.BlockSpec(memory_space=pltpu.SMEM)
    bf16, f32 = jnp.bfloat16, jnp.float32
    return pl.pallas_call(
        layer_kernel,
        out_shape=(
            jax.ShapeDtypeStruct(tokens.shape, bf16),
            jax.ShapeDtypeStruct((reqs, toks, 2 * heads * HD), bf16),
        ),
        in_specs=[smem, smem, smem, hbm, hbm, hbm, hbm, vmem, vmem],
        out_specs=(vmem, hbm),
        scratch_shapes=[
            pltpu.VMEM((owners, toks, width), bf16),
            pltpu.VMEM((owners, 4, w_qkv.shape[0] // 4, 3 * HD), bf16),
            pltpu.VMEM((2, rows, HD), bf16),
            pltpu.VMEM((owners, toks, 2 * HD), bf16),
            pltpu.VMEM((slots, heads, page, 2 * HD), bf16),
            pltpu.VMEM((planes, owners) + w_out.shape, bf16),
            pltpu.VMEM((2,) + w_out.shape, bf16),
            pltpu.VMEM((page_table.shape[1], page, rows // 2), f32),
            pltpu.VMEM((2, rows // page, page, rows // 2), f32),
            pltpu.VMEM((2, 8, rows // 2), f32),
            pltpu.VMEM((2, 8, rows // 2), f32),
            pltpu.VMEM((2, HD, rows // 2), f32),
            pltpu.VMEM((8, rows // 2), f32),
            pltpu.VMEM((8, rows // 2), f32),
            pltpu.VMEM((HD, rows // 2), f32),
            pltpu.VMEM((2, HD, rows // 2), bf16),
            pltpu.VMEM((2, 8, rows // 2), f32),
            pltpu.VMEM((2, HD, rows // 2), bf16),
            pltpu.VMEM((2, 8, rows // 2), f32),
            pltpu.VMEM((owners, toks, HD), bf16),
            pltpu.VMEM((reqs, toks, heads * HD), bf16),
            pltpu.VMEM((reqs * toks, width), f32),
            pltpu.VMEM(tokens.shape, bf16),
            dma((15, 2)),
            dma((owners, 2)),
            dma((planes, 3)),
            dma((heads, 3)),
            dma((7,)),
            dma((4, 2)),
            dma((heads, 2)),
            dma((heads, 2)),
            dma((6,)),
            dma((4, 2)),
            dma((owners, 2)),
            dma((owners, 2)),
            dma((2,)),
            dma((2,)),
            dma((7,)),
            dma,
            dma,
            dma((owners,)),
            dma((2,)),
            dma((14,)),
            dma((planes, 2)),
            dma((2, 2)),
            dma((2, 2)),
            dma((owners,)),
            dma((owners,)),
        ],
        compiler_params=pltpu.CompilerParams(
            collective_id=0, has_side_effects=True, vmem_limit_bytes=67043328
        ),
        name="layer",
    )(
        page_table,
        prefix_len,
        group_of,
        tokens,
        w_qkv,
        w_out,
        kv_pool,
        ln_gain.reshape(1, width),
        ln_bias.reshape(1, width),
    )


def solution(mesh):
    in_specs = (
        P("dp", "fsdp", None),
        P("fsdp", "dp"),
        P("fsdp", "dp"),
        P(),
        P(),
        P("fsdp", None, None),
        P(),
        P(),
        P("dp"),
    )
    out_specs = (P("dp", "fsdp", None), P("dp", "fsdp", None))
    return jax.shard_map(body, mesh=mesh, in_specs=in_specs, out_specs=out_specs, check_vma=False)
```
